256 devices in a mesh: gx: 8 (over x, core), gy: 16 (over y_hi, z), gz: 2 (over y_lo).
Axes of the slice: x: 4, y: 4 (y_hi: 2, y_lo: 2; y = y_hi * 2 + y_lo), z: 8, core: 2. Of those that a mesh axis runs over, the one named last changes fastest.
Arguments:
- fields: float32 [4, 64, 512, 256], P(None, 'gx', 'gy', 'gz'), may hold values from -6 to 6
- viscosity: float32 [64, 512, 256], P('gx', 'gy', 'gz'), may hold values from 0.02 to 0.6
- samples: int32 [8, 16, 2, 8], P('gx', 'gy', 'gz'), may hold values from 0 to 511
- trainers: int32 [8, 16, 2, 8, 1], P('gx', 'gy', 'gz'), may hold values from 0 to 15; in each aligned block of 8 rows (0 to 7, 8 to 15, ..., all dimensions but the last counted through in order) at most 2 rows name the same one
- conv_first: bfloat16 [32, 108], replicated, may hold values from -0.625 to 0.625
- conv_second: bfloat16 [32, 864], replicated, may hold values from -0.21875 to 0.21875
- conv_third: bfloat16 [6, 32], replicated, may hold values from -1 to 1
Outputs:
- advanced: float32 [4, 64, 512, 256], P(None, 'gx', 'gy', 'gz')
- block_losses: float32 [8, 16, 2, 32], P('gx', 'gy', 'gz')
- first_grad: float32 [32, 108], replicated
- second_grad: float32 [32, 864], replicated
- third_grad: float32 [6, 32], replicated
The draws below stay inside these ranges and needn't reach their ends.
Inputs may be any that keep to these rules, and one draw needn't show every extreme that they name: `trainers`: among the 8 samples of one device no trainer occurs more than 2 times, and on some device one occurs exactly 2 times.
All inputs are finite; a program needn't handle non-finite values.
Results may differ from the reference program's by a relative error of at most 0.0036.
The reference program's roundings to bfloat16 on the way (of `chosen`, `stack`, `hidden_first`, `hidden_second`, `grad_pred`, `grad_mid` and `grad_entry`) count: a program that leaves them out, or rounds other values in their place, can miss the bound.
Values may be sent and summed in bfloat16 or wider, within the bound.
A program may use at most 128 MiB of HBM per device.

```python
import math
from functools import reduce
import jax
import jax.numpy as jnp
import numpy as np
from jax import lax

CX = 8
CY = 32
CZ = 128
SAMP = 8
BLK = 4
CAP = 2
NF = 4
NOUT = 6
CH = 32
NX = 64
NY = 512
NZ = 256
NB = 512
SLOTS = 32
WORKERS = 256
N_GX = 8
N_GY = 16
N_GZ = 2


def place_ends(entries, key, smallest, high):
    dims = entries.shape
    index_at = [jax.random.randint(jax.random.fold_in(key, axis), (), 0, dims[axis]) for axis in range(len(dims))]
    entries = entries.at[tuple(index_at)].set(smallest)
    longest = dims.index(max(dims))
    index_at[longest] = (index_at[longest] + 1) % dims[longest]
    return entries.at[tuple(index_at)].set(high)


def levels(key, extent, split, smallest, largest):
    def one(position, parts):
        heights = jax.random.uniform(jax.random.fold_in(jax.random.fold_in(key, 6), position), (parts,), jnp.float32, smallest / len(split), largest / len(split))
        return jnp.repeat(jnp.exp(heights), extent[position] // parts).reshape((-1,) + (1,) * (len(extent) - position - 1))

    gain = one(*split[0])
    for cut in split[1:]:
        gain = gain * one(*cut)
    return gain


def deal_out(own_key, own, number, rows, amount, top, bound, skew):
    order = jax.random.permutation(own_key, amount)
    packed, ordinary = shares(amount, rows * top, bound, skew, True), shares(amount, rows * top, bound, skew, False)
    places = jnp.arange(amount)

    def named(tallies, turn):
        used = int((tallies > 0).sum())
        fixed = max(1, used // 4)
        shifted = fixed + (places - fixed + turn * (used - fixed)) % max(1, amount - fixed)
        return jnp.zeros((amount,), jnp.int32).at[order[jnp.where(places < fixed, places, shifted)]].set(jnp.asarray(tallies, jnp.int32))

    tallies = jnp.where(number % 4 == 0, named(packed, number // 4), named(ordinary, number - number // 4 - 1))
    mixed = jax.random.permutation(jax.random.fold_in(own, 3), amount)
    donor, sink = mixed[0:amount // 2 * 2:2], mixed[1:amount // 2 * 2:2]
    room = jnp.minimum(tallies[donor] - 1, bound - tallies[sink]) // 2
    room = jnp.where((donor == order[0]) | (sink == order[0]) | (tallies[sink] == 0), 0, jnp.maximum(room, 0))
    shifted = jax.random.randint(jax.random.fold_in(own, 4), (amount // 2,), 0, 1 << 20) % (room + 1)
    tallies = tallies.at[donor].add(-shifted).at[sink].add(shifted)
    items = jnp.searchsorted(jnp.cumsum(tallies), jnp.arange(rows * top), side="right").astype(jnp.int32)
    table = items.reshape(top, rows).T
    table = table[jax.random.permutation(jax.random.fold_in(own, 1), rows)]
    turn = jax.random.randint(jax.random.fold_in(own, 2), (rows, 1), 0, top)
    return jnp.take_along_axis(table, (jnp.arange(top)[None, :] + turn) % top, axis=1)


def shares(number_of, total, most, lean, full):
    weights = [(1 << 20) // math.isqrt(standing ** lean) + 1 for standing in range(1, number_of + 1)]
    largest = most if full else min(most, max(-(-total // number_of), total * weights[0] // sum(weights)))
    least = 1 if total - largest >= number_of - 1 else 0
    given, surplus = [largest] + [least] * (number_of - 1), total - largest - least * (number_of - 1)
    while surplus > 0:
        free = [i for i in range(1, number_of) if given[i] < largest] or [i for i in range(1, number_of) if given[i] < most]
        mass, remaining = sum([weights[i] for i in free]), surplus
        for i in free:
            more = min(most - given[i], max(1, remaining * weights[i] // mass), surplus)
            given[i] = given[i] + more
            surplus = surplus - more
    return np.array(given)


def gaussian(stream_key, extent, scale, most, split=(), kind=jnp.bfloat16):
    factor_of = levels(stream_key, extent, split, -0.22, 0.18) if split else 1.0
    values = jax.random.normal(stream_key, extent, jnp.float32) * scale * factor_of
    return jnp.minimum(jnp.maximum(values, -most), most).astype(kind)


def setup_inputs(seed: int = 0) -> dict:
    key_list = jax.random.split(jax.random.key(seed), 8)
    fields = gaussian(key_list[0], (NF, NX, NY, NZ), 1.0, 6.0, ((1, 8), (2, 16), (3, 2)), jnp.float32)
    viscosity = jnp.clip(jnp.exp(math.log(0.6) - 3.4011974 * jax.random.uniform(key_list[1], (NX, NY, NZ), jnp.float32) ** levels(key_list[1], (NX, NY, NZ), ((0, 8), (1, 16), (2, 2)), -0.2, 0.2)), 0.02, 0.6)
    samples = place_ends(jax.random.randint(key_list[2], (N_GX, N_GY, N_GZ, SAMP), 0, NB), jax.random.fold_in(key_list[2], 1), 0, NB - 1).astype(jnp.int32)
    trainers_keys = jax.random.split(jax.random.fold_in(key_list[3], 1), N_GX * N_GY * N_GZ * SAMP // SAMP)
    trainers_turns = jax.random.permutation(jax.random.fold_in(key_list[3], 3), N_GX * N_GY * N_GZ * SAMP // SAMP)
    trainers = jax.vmap(lambda own, number: deal_out(jax.random.fold_in(key_list[3], 2), own, number, SAMP, N_GY, 1, CAP, 2))(trainers_keys, trainers_turns).reshape((N_GX, N_GY, N_GZ, SAMP, 1))
    conv_first = gaussian(key_list[4], (CH, 27 * NF), (27 * NF) ** -0.5, 0.625)
    conv_second = gaussian(key_list[5], (CH, 27 * CH), (27 * CH) ** -0.5, 0.21875)
    conv_third = gaussian(key_list[6], (NOUT, CH), CH ** -0.5, 1.0)
    return dict(fields=fields, viscosity=viscosity, samples=samples, trainers=trainers, conv_first=conv_first, conv_second=conv_second, conv_third=conv_third)


time_step = 0.25
buoyancy = 0.5


def advance(fields, viscosity):
    summed_div = None
    for dimension in range(3):
        ahead = jnp.roll(fields, -1, dimension + 1)
        face_speed = fields[dimension] + ahead[dimension]
        face_visc = viscosity + jnp.roll(viscosity, -1, dimension)
        face_flux = 0.25 * face_speed * (fields + ahead) - 0.5 * face_visc * (ahead - fields)
        diverge = face_flux - jnp.roll(face_flux, 1, dimension + 1)
        summed_div = diverge if summed_div is None else summed_div + diverge
    updated = fields - time_step * summed_div
    return updated.at[2].add(time_step * buoyancy * fields[3])


def shifted_copies(values, block_edge, direction):
    length = values.shape[-1]
    within = jnp.arange(length, dtype=jnp.int32) % (block_edge * block_edge * block_edge)
    coord_x = within // (block_edge * block_edge)
    coord_y = (within // block_edge) % block_edge
    coord_z = within % block_edge
    pieces = []
    for step_x in (-1, 0, 1):
        for step_y in (-1, 0, 1):
            for step_z in (-1, 0, 1):
                move_x = direction * step_x
                move_y = direction * step_y
                move_z = direction * step_z
                inside = ((coord_x + move_x >= 0) & (coord_x + move_x < block_edge)
                          & (coord_y + move_y >= 0) & (coord_y + move_y < block_edge)
                          & (coord_z + move_z >= 0) & (coord_z + move_z < block_edge))
                rolled = jnp.roll(values, -(move_x * block_edge * block_edge + move_y * block_edge + move_z), axis=1)
                pieces.append(jnp.where(inside[None, :], rolled, jnp.zeros_like(rolled)))
    return pieces


def silu_slope(values):
    sigmoid_v = jax.nn.sigmoid(values)
    return sigmoid_v * (1.0 + values * (1.0 - sigmoid_v))


def subgrid_stress(fields, block_edge):
    velocity = fields[:3]
    products = jnp.stack([velocity[0] * velocity[0], velocity[1] * velocity[1], velocity[2] * velocity[2],
                          velocity[0] * velocity[1], velocity[0] * velocity[2], velocity[1] * velocity[2]])
    joined = jnp.concatenate([velocity, products], 0)
    filtered = reduce(jnp.add, shifted_copies(joined, block_edge, 1)) / 27.0
    smooth = filtered[:3]
    return filtered[3:] - jnp.stack([smooth[0] * smooth[0], smooth[1] * smooth[1], smooth[2] * smooth[2],
                                     smooth[0] * smooth[1], smooth[0] * smooth[2], smooth[1] * smooth[2]])


def closure_step(inputs, slot_weight, conv_first, conv_second, conv_third, block_edge):
    volume = block_edge ** 3
    slots_here = inputs.shape[1] // volume
    contract = (((1,), (1,)), ((), ()))
    stack_in = jnp.concatenate(shifted_copies(inputs, block_edge, 1), 0)
    pre_first = jnp.dot(conv_first, stack_in, preferred_element_type=jnp.float32)
    hidden_first = jax.nn.silu(pre_first).astype(jnp.bfloat16)
    stack_mid = jnp.concatenate(shifted_copies(hidden_first, block_edge, 1), 0)
    pre_second = jnp.dot(conv_second, stack_mid, preferred_element_type=jnp.float32)
    hidden_second = jax.nn.silu(pre_second).astype(jnp.bfloat16)
    predicted = jnp.dot(conv_third, hidden_second, preferred_element_type=jnp.float32)
    target = subgrid_stress(inputs.astype(jnp.float32), block_edge)
    misfit = predicted - target
    out_rows = misfit.shape[0]
    shaped = misfit.reshape(out_rows, slots_here, volume)
    losses = jnp.sum(shaped * shaped, axis=(0, 2)) / (out_rows * volume)
    scale_slot = slot_weight * (2.0 / (out_rows * volume))
    grad_pred = (shaped * scale_slot[None, :, None]).reshape(misfit.shape).astype(jnp.bfloat16)
    grad_third = lax.dot_general(grad_pred, hidden_second, contract, preferred_element_type=jnp.float32)
    grad_upper = lax.dot_general(conv_third, grad_pred, (((0,), (0,)), ((), ())), preferred_element_type=jnp.float32)
    grad_mid = (grad_upper * silu_slope(pre_second)).astype(jnp.bfloat16)
    grad_second = lax.dot_general(grad_mid, stack_mid, contract, preferred_element_type=jnp.float32)
    back_stack = jnp.concatenate(shifted_copies(grad_mid, block_edge, -1), 0)
    channels = conv_second.shape[0]
    turned = conv_second.reshape(channels, 27, channels).transpose(2, 1, 0).reshape(channels, 27 * channels)
    grad_lower = jnp.dot(turned, back_stack, preferred_element_type=jnp.float32)
    grad_entry = (grad_lower * silu_slope(pre_first)).astype(jnp.bfloat16)
    grad_first = lax.dot_general(grad_entry, stack_in, contract, preferred_element_type=jnp.float32)
    return losses, (grad_first, grad_second, grad_third)


def reference(fields, viscosity, samples, trainers, conv_first, conv_second, conv_third):
    middle = advance(fields, viscosity)
    advanced = advance(middle, viscosity)
    volume = BLK ** 3
    blocks = advanced.reshape(NF, NX // BLK, BLK, NY // BLK, BLK, NZ // BLK, BLK)
    blocks = blocks.transpose(0, 1, 3, 5, 2, 4, 6).reshape(NF, NX // BLK, NY // BLK, NZ // BLK, volume)
    local_x = CX // BLK
    local_y = CY // BLK
    local_z = CZ // BLK
    pos_x = jnp.arange(N_GX, dtype=jnp.int32).reshape(N_GX, 1, 1, 1)
    pos_y = jnp.arange(N_GY, dtype=jnp.int32).reshape(1, N_GY, 1, 1)
    pos_z = jnp.arange(N_GZ, dtype=jnp.int32).reshape(1, 1, N_GZ, 1)
    block_x = pos_x * local_x + samples // (local_y * local_z)
    block_y = pos_y * local_y + (samples // local_z) % local_y
    block_z = pos_z * local_z + samples % local_z
    chosen = blocks[:, block_x, block_y, block_z].astype(jnp.bfloat16)
    owners = trainers[..., 0]
    owner_hot = (owners[..., None] == jnp.arange(N_GY, dtype=jnp.int32)).astype(jnp.float32)
    load_sums = jnp.sum(owner_hot, axis=(1, 3))
    load_of = jnp.sum(owner_hot * load_sums[:, None, :, None, :], axis=-1)
    sample_share = 1.0 / (WORKERS * jnp.maximum(load_of, 1.0))
    positions = jnp.arange(SAMP, dtype=jnp.int32)
    earlier = (owners[..., :, None] == owners[..., None, :]) & (positions[:, None] < positions[None, :])
    rank_of = jnp.sum(earlier.astype(jnp.int32), axis=-2)
    batched = chosen.reshape(NF, WORKERS, SAMP, volume).transpose(1, 0, 2, 3)
    weights = sample_share.reshape(WORKERS, SAMP)

    def per_device(summed, device_items):
        inputs, weight_here = device_items
        losses, gradients = closure_step(inputs.reshape(NF, SAMP * volume), weight_here,
                                         conv_first, conv_second, conv_third, BLK)
        return jax.tree.map(jnp.add, summed, gradients), losses

    starting = (jnp.zeros((CH, 27 * NF), jnp.float32), jnp.zeros((CH, 27 * CH), jnp.float32),
                jnp.zeros((NOUT, CH), jnp.float32))
    summed, losses = lax.scan(per_device, starting, (batched, weights))
    shape_four = (N_GX, N_GY, N_GZ, SAMP)
    index_x = jnp.broadcast_to(pos_x, shape_four)
    index_y = jnp.broadcast_to(pos_y, shape_four)
    index_z = jnp.broadcast_to(pos_z, shape_four)
    slot_losses = jnp.zeros((N_GX, N_GY, N_GZ, SLOTS), jnp.float32)
    slot_losses = slot_losses.at[index_x, owners, index_z, index_y * CAP + rank_of].set(losses.reshape(shape_four))
    return advanced, slot_losses, summed[0], summed[1], summed[2]
```

```python
import jax
import jax.numpy as jnp
from jax import lax
from jax.experimental import pallas as pl
from jax.experimental.pallas import tpu as pltpu
from jax.sharding import PartitionSpec as P

MESH = pl.DeviceIdType.MESH
F32 = jnp.float32
BF16 = jnp.bfloat16
I32 = jnp.int32
HIGH = lax.Precision.HIGHEST

NX, NY, NZ = 8, 16, 2
WORKERS = NX * NY * NZ
NT = (((1,), (1,)), ((), ()))
TN = (((0,), (0,)), ((), ()))
TIME_STEP = 0.25
BUOYANCY = 0.5
PAIR_P = (0, 1, 2, 0, 0, 1)
PAIR_Q = (0, 1, 2, 1, 2, 2)


def iota(shape, dim):
    return lax.broadcasted_iota(I32, shape, dim)


def flux(low, high, visc_low, visc_high, d):
    speed = 0.25 * (low[d] + high[d])
    visc = 0.5 * (visc_low + visc_high)
    return [speed * (a + b) - visc * (b - a) for a, b in zip(low, high)]


def advance_plane(src, visc, halo_y, visc_y, halo_z, p):
    rows = iota((32, 128), 0)
    lanes = iota((32, 128), 1)
    q = [src[c, p] for c in range(4)]
    v = visc(p)
    q_before = [src[c, p - 1] for c in range(4)]
    q_after = [src[c, p + 1] for c in range(4)]
    total = [
        a - b
        for a, b in zip(flux(q, q_after, v, visc(p + 1), 0), flux(q_before, q, visc(p - 1), v, 0))
    ]
    at = pl.ds(p - 1, 1)
    y_low = [halo_y[0, c, at] for c in range(4)]
    y_high = [halo_y[1, c, at] for c in range(4)]

    def up(x, edge):
        return jnp.where(rows == 31, edge, pltpu.roll(x, 31, 0))

    q_next = [up(x, e) for x, e in zip(q, y_high)]
    faces = flux(q, q_next, v, up(v, visc_y[1, 4, at]), 1)
    first = flux(y_low, [x[0:1] for x in q], visc_y[0, 4, at], v[0:1], 1)
    total = [
        t + (f - jnp.where(rows == 0, e, pltpu.roll(f, 1, 0)))
        for t, f, e in zip(total, faces, first)
    ]
    side = [halo_z[c, p - 1] for c in range(4)]
    side_v = halo_z[4, p - 1]

    def along(x, edge):
        return jnp.where(lanes == 127, edge, pltpu.roll(x, 127, 1))

    q_next = [along(x, e) for x, e in zip(q, side)]
    faces = flux(q, q_next, v, along(v, side_v), 2)
    first = flux(side, q, side_v, v, 2)
    total = [
        t + (f - jnp.where(lanes == 0, e, pltpu.roll(f, 1, 1)))
        for t, f, e in zip(total, faces, first)
    ]
    out = [x - TIME_STEP * t for x, t in zip(q, total)]
    out[2] = out[2] + (TIME_STEP * BUOYANCY) * q[3]
    return out


def pack_sides(src, count, y_send, z_send):
    for c in range(count):
        y_send[0, c] = src[c, 1:9, 0, :]
        y_send[1, c] = src[c, 1:9, 31, :]
        for h in range(2):
            turned = src[c, 1 + 4 * h : 5 + 4 * h].reshape(128, 128).T
            g = 2 * c + h
            z_send[0, g : g + 1, :] = turned[0:1]
            z_send[1, g : g + 1, :] = turned[127:128]


def unpack_sides(z_recv, count, halo_z):
    rows = iota((128, 128), 0)
    for c in range(count):
        for h in range(2):
            g = 2 * c + h
            first = z_recv[0, g : g + 1, :]
            last = z_recv[1, g : g + 1, :]
            placed = jnp.where(rows == 0, last, jnp.where(rows == 127, first, 0.0))
            halo_z[c, 4 * h : 4 * h + 4] = placed.T.reshape(4, 32, 128)


def by_lane(values, lanes_of):
    out = jnp.zeros(lanes_of.shape, I32)
    for j in range(8):
        out = jnp.where(lanes_of == j, values[j], out)
    return out


def shifts():
    return [(ox, oy) for ox in (-1, 0, 1) for oy in (-1, 0, 1)]


def inside(shape, ox, oy):
    lanes = iota(shape, 1)
    x = lanes // 4 % 4 + ox
    y = lanes % 4 + oy
    return (x >= 0) & (x < 4) & (y >= 0) & (y < 4)


def rolled(x, ox, oy):
    if ox == 0 and oy == 0:
        return x
    moved = pltpu.roll(x, (-(4 * ox + oy)) % 128, 1)
    return jnp.where(inside(x.shape, ox, oy), moved, 0.0)


def box(x):
    rows = iota(x.shape, 0) % 4
    lanes = iota(x.shape, 1)
    count = x.shape[0]
    x = (
        x
        + jnp.where(rows > 0, pltpu.roll(x, 1, 0), 0.0)
        + jnp.where(rows < 3, pltpu.roll(x, count - 1, 0), 0.0)
    )
    for step, place in ((1, lanes % 4), (4, lanes // 4 % 4)):
        x = (
            x
            + jnp.where(place > 0, pltpu.roll(x, step, 1), 0.0)
            + jnp.where(place < 3, pltpu.roll(x, 128 - step, 1), 0.0)
        )
    return x / 27.0


def cat_rows(x):
    return jnp.concatenate([x[:, 128 * z : 128 * z + 128] for z in range(4)], axis=0)


def dot(a, b, dims=None, precision=None):
    if dims is None:
        dims = (((1,), (0,)), ((), ()))
    return lax.dot_general(a, b, dims, precision=precision, preferred_element_type=F32)


def whole_kernel(
    fields_hbm, visc_hbm, samples, trainers, w1_hbm, w2_hbm, w3_hbm,
    adv_hbm, loss_out, first_out, second_out, third_out,
    start, mid, adv, y_send, y_recv, z_send, z_recv, y_send2, y_recv2, z_send2, z_recv2,
    halo_z, t_send, t_recv, l_send, l_recv, w1, w2, w3, st1, st2,
    grads, part, sum1, spread, sum2, final,
    local_sem, x_s, x_r, y_s, y_r, z_s, z_r, x2_s, x2_r, y2_s, y2_r, z2_s, z2_r,
    t_s, t_r, l_s, l_r, a_s, a_r, b_s, b_r, c_s, c_r,
):
    ax = lax.axis_index("gx")
    ay = lax.axis_index("gy")
    az = lax.axis_index("gz")
    aw = ax * NZ + az

    def in_y(d):
        return (ax, lax.rem(ay + d, NY), az)

    def in_w(d):
        w = lax.rem(aw + d, NX * NZ)
        return (w // NZ, ay, lax.rem(w, NZ))

    loads = [
        pltpu.make_async_copy(fields_hbm, start.at[0:4, 1:9], local_sem.at[0]),
        pltpu.make_async_copy(visc_hbm, start.at[4, 1:9], local_sem.at[1]),
        pltpu.make_async_copy(w1_hbm, w1, local_sem.at[2]),
        pltpu.make_async_copy(w2_hbm, w2, local_sem.at[3]),
        pltpu.make_async_copy(w3_hbm, w3, local_sem.at[4]),
    ]
    for load in loads:
        load.start()

    barrier = pltpu.get_barrier_semaphore()

    def greet(d, carry):
        pl.semaphore_signal(barrier, inc=1, device_id=in_y(d), device_id_type=MESH)
        pl.semaphore_signal(barrier, inc=1, device_id=in_w(d), device_id_type=MESH)
        return carry

    lax.fori_loop(1, 16, greet, 0)
    picked = [samples[j] for j in range(8)]
    owners = [trainers[j] for j in range(8)]
    t_send[...] = by_lane(owners, iota((1, 128), 1) % 8)
    loads[0].wait()
    loads[1].wait()
    pl.semaphore_wait(barrier, 30)

    def remote(src, dst, s, r, to):
        return pltpu.make_async_remote_copy(
            src_ref=src, dst_ref=dst, send_sem=s, recv_sem=r, device_id=to, device_id_type=MESH
        )

    x_up = (lax.rem(ax + 1, NX), ay, az)
    x_down = (lax.rem(ax + NX - 1, NX), ay, az)
    other = (ax, ay, 1 - az)

    def exchange_x(ref, s, r):
        return [
            remote(ref.at[:, 8], ref.at[:, 0], s.at[0], r.at[0], x_up),
            remote(ref.at[:, 1], ref.at[:, 9], s.at[1], r.at[1], x_down),
        ]

    def exchange_yz(ys, yr, zs, zr, ysem, yrem, zsem, zrem):
        return [
            remote(ys.at[1], yr.at[0], ysem.at[0], yrem.at[0], in_y(1)),
            remote(ys.at[0], yr.at[1], ysem.at[1], yrem.at[1], in_y(NY - 1)),
            remote(zs, zr, zsem, zrem, other),
        ]

    moves = exchange_x(start, x_s, x_r)
    for move in moves:
        move.start()
    pack_sides(start, 5, y_send, z_send)
    sides = exchange_yz(y_send, y_recv, z_send, z_recv, y_s, y_r, z_s, z_r)
    for move in sides:
        move.start()

    def everyone(src, buf, s, r, slot, to):
        def begin(d, carry):
            remote(src, buf.at[slot], s.at[d], r.at[slot], to(d)).start()
            return carry

        lax.fori_loop(1, 16, begin, 0)

    def all_here(src, buf, s, r, slot, to):
        def finish(d, carry):
            at = lax.rem(slot + d, 16)
            copy = remote(src, buf.at[at], s.at[d], r.at[at], to(d))
            copy.wait_send()
            copy.wait_recv()
            return carry

        lax.fori_loop(1, 16, finish, 0)

    everyone(t_send, t_recv, t_s, t_r, ay, in_y)
    t_recv[ay] = t_send[...]

    for move in sides:
        move.wait()
    unpack_sides(z_recv, 5, halo_z)
    for move in moves:
        move.wait()

    def visc(p):
        return start[4, p]

    def store_mid(p):
        for c, x in enumerate(advance_plane(start, visc, y_recv, y_recv, halo_z, p)):
            mid[c, p] = x

    store_mid(1)
    store_mid(8)
    moves = exchange_x(mid, x2_s, x2_r)
    for move in moves:
        move.start()

    def first_step(p, carry):
        store_mid(p)
        return carry

    lax.fori_loop(2, 8, first_step, 0)
    pack_sides(mid, 4, y_send2, z_send2)
    sides = exchange_yz(y_send2, y_recv2, z_send2, z_recv2, y2_s, y2_r, z2_s, z2_r)
    for move in sides:
        move.start()
    for move in sides:
        move.wait()
    unpack_sides(z_recv2, 4, halo_z)

    def store_adv(p):
        for c, x in enumerate(advance_plane(mid, visc, y_recv2, y_recv, halo_z, p)):
            adv[c, p - 1] = x

    def second_step(p, carry):
        store_adv(p)
        return carry

    lax.fori_loop(2, 8, second_step, 0)
    for move in moves:
        move.wait()
    store_adv(1)
    store_adv(8)
    write = pltpu.make_async_copy(adv, adv_hbm, local_sem.at[5])
    write.start()

    row = iota((128, 256), 0)
    base = by_lane([(s // 256) * 128 + (s // 32 % 8) * 4 for s in picked], row // 16)
    want = base + row // 4 % 4 * 32 + row % 4
    hot = jnp.where(want == iota((128, 256), 1), 1.0, 0.0).astype(BF16)
    lanes128 = iota((128, 128), 1)
    keep = by_lane([s % 32 for s in picked], iota((128, 128), 0) // 16) == lanes128 // 4
    frow = iota((64, 128), 0)
    flane = iota((64, 128), 1)
    comp = frow % 4
    zrow = frow // 4
    for i, c in enumerate(PAIR_P + PAIR_Q):
        here = (frow >= 16 + 4 * i) & (frow < 20 + 4 * i)
        comp = jnp.where(here, c, comp)
    zrow = jnp.where(frow < 16, zrow, frow % 4)
    cells = jnp.zeros((64, 128), F32)
    for c in range(4):
        plane = adv[c].reshape(256, 128).astype(BF16)
        found = jnp.where(keep, dot(hot, plane), 0.0).astype(BF16)
        fold = jnp.where((comp == c) & (flane % 4 == zrow), 1.0, 0.0).astype(BF16)
        cells = cells + dot(fold, found, NT)

    loads[2].wait()
    loads[3].wait()
    loads[4].wait()
    st1[...] = jnp.zeros_like(st1)
    chosen = cells[0:16]
    for i, (ox, oy) in enumerate(shifts()):
        moved = rolled(chosen, ox, oy)
        for o in range(3):
            k = 3 * i + o
            for z in range(4):
                if 0 <= z + o - 1 < 4:
                    st1[4 * k : 4 * k + 4, 128 * z : 128 * z + 128] = moved[
                        4 * (z + o - 1) : 4 * (z + o - 1) + 4
                    ]
    pre1 = cat_rows(dot(w1[...], st1[0:108, :].astype(BF16)))
    sig1 = jax.nn.sigmoid(pre1)
    slope1 = sig1 * (1.0 + pre1 * (1.0 - sig1))
    hid1 = (pre1 * sig1).astype(BF16).astype(F32)
    for i, (ox, oy) in enumerate(shifts()):
        moved = rolled(hid1, ox, oy).astype(BF16)
        for o in range(3):
            k = 3 * i + o
            for z in range(4):
                if 0 <= z + o - 1 < 4:
                    piece = moved[32 * (z + o - 1) : 32 * (z + o)]
                else:
                    piece = jnp.zeros((32, 128), BF16)
                st2[32 * k : 32 * k + 32, 128 * z : 128 * z + 128] = piece
    pre2 = cat_rows(dot(w2[...], st2[0:864, :]))
    sig2 = jax.nn.sigmoid(pre2)
    slope2 = sig2 * (1.0 + pre2 * (1.0 - sig2))
    hid2 = (pre2 * sig2).astype(BF16)
    pick_row = jnp.where(iota((24, 6), 0) // 4 == iota((24, 6), 1), 1.0, 0.0).astype(BF16)
    pick_col = jnp.where(iota((32, 128), 1) % 32 == iota((32, 128), 0), 1.0, 0.0).astype(BF16)
    spread3 = dot(dot(pick_row, w3[...]).astype(BF16), pick_col)
    same_z = iota((24, 128), 0) % 4 == iota((24, 128), 1) // 32
    wide3 = jnp.where(same_z, spread3, 0.0).astype(BF16)
    predicted = dot(wide3, hid2)
    up_p, up_q = cells[16:40], cells[40:64]
    target = box(up_p * up_q) - box(up_p) * box(up_q)
    misfit = predicted - target

    squares = jnp.broadcast_to(jnp.sum(misfit * misfit, axis=0, keepdims=True), (8, 128))
    group = jnp.where(iota((128, 128), 0) // 16 == lanes128 % 8, 1.0, 0.0)
    l_send[...] = dot(squares, group, precision=HIGH)[0:1] / 384.0
    all_here(t_send, t_recv, t_s, t_r, ay, in_y)
    everyone(l_send, l_recv, l_s, l_r, ay, in_y)
    l_recv[ay] = l_send[...]
    owned = t_recv[:, 0, :]
    mine = by_lane(owners, iota((16, 128), 1) // 16)
    load = jnp.zeros((16, 128), F32)
    for s in range(8):
        other_owner = owned if s == 0 else pltpu.roll(owned, s, 1)
        load = load + jnp.where(other_owner == mine, 1.0, 0.0)
    load = jnp.sum(load, axis=0, keepdims=True)
    share = 1.0 / (WORKERS * jnp.maximum(load, 1.0))
    grad_pred = (misfit * (share * (2.0 / 384.0))).astype(BF16)

    third = jnp.where(same_z, dot(grad_pred, hid2, NT), 0.0)
    third = jnp.concatenate(
        [jnp.sum(third[4 * i : 4 * i + 4], axis=0, keepdims=True) for i in range(6)]
        + [jnp.zeros((26, 128), F32)],
        axis=0,
    )
    third = third + pltpu.roll(third, 32, 1)
    third = third + pltpu.roll(third, 64, 1)
    grad_mid = (dot(wide3, grad_pred, TN) * slope2).astype(BF16)
    mid_cols = jnp.concatenate([grad_mid[32 * z : 32 * z + 32] for z in range(4)], axis=1)

    def send_tile(i):
        for h in range(2):
            to = 2 * i + h

            @pl.when(ay != to)
            def _():
                remote(grads.at[to], part.at[ay], a_s.at[to], a_r.at[ay], (ax, to, az)).start()

    def store_tile(i, x):
        grads[2 * i] = x[0:16]
        grads[2 * i + 1] = x[16:32]

    for i in range(7):
        rows_here = 128 if i < 6 else 96
        tile = dot(mid_cols, st2[128 * i : 128 * i + rows_here, :], NT)
        if i == 6:
            tile = jnp.concatenate([tile, third[:, 96:128]], axis=1)
        store_tile(i, tile)
        send_tile(i)
    lower = jnp.zeros((128, 128), F32)
    for i, (ox, oy) in enumerate(shifts()):
        y = dot(w2[:, 96 * i : 96 * i + 96], mid_cols, TN)
        parts = []
        for z in range(4):
            total = y[32:64, 128 * z : 128 * z + 128]
            if z + 1 < 4:
                total = total + y[0:32, 128 * z + 128 : 128 * z + 256]
            if z - 1 >= 0:
                total = total + y[64:96, 128 * z - 128 : 128 * z]
            parts.append(total)
        lower = lower + rolled(jnp.concatenate(parts, axis=0), -ox, -oy)
    entry = (lower * slope1).astype(BF16)
    entry_cols = jnp.concatenate([entry[32 * z : 32 * z + 32] for z in range(4)], axis=1)
    store_tile(7, dot(entry_cols, st1[...].astype(BF16), NT))
    send_tile(7)

    part[ay] = grads[ay]
    for to in range(16):

        @pl.when(ay != to)
        def _():
            remote(grads.at[to], part.at[to], a_s.at[to], a_r.at[to], (ax, to, az)).wait()

    def added(buf):
        total = buf[0]
        for s in range(1, 16):
            total = total + buf[s]
        return total

    sum1[...] = added(part)
    everyone(sum1, spread, b_s, b_r, aw, in_w)
    spread[aw] = sum1[...]
    all_here(sum1, spread, b_s, b_r, aw, in_w)
    sum2[...] = added(spread)
    everyone(sum2, final, c_s, c_r, ay, in_y)
    final[ay] = sum2[...]

    all_here(l_send, l_recv, l_s, l_r, ay, in_y)
    lanes16 = iota((16, 128), 1)
    rank = jnp.zeros((16, 128), I32)
    for s in range(1, 8):
        earlier = (pltpu.roll(owned, s, 1) == owned) & (lanes16 % 8 >= s)
        rank = rank + jnp.where(earlier, 1, 0)
    losses = l_recv[:, 0, :]
    own = (owned == ay) & (lanes16 < 8)
    place = lanes16 - 2 * iota((16, 128), 0)
    slots = jnp.zeros((16, 128), F32)
    for r in range(2):
        value = jnp.sum(jnp.where(own & (rank == r), losses, 0.0), axis=1, keepdims=True)
        slots = slots + jnp.where(place == r, value, 0.0)
    loss_out[...] = jnp.sum(slots, axis=0, keepdims=True)[:, 0:32]

    all_here(sum2, final, c_s, c_r, ay, in_y)
    for i in range(6):
        second_out[:, 128 * i : 128 * i + 128] = final[2 * i : 2 * i + 2].reshape(32, 128)
    last = final[12:14].reshape(32, 128)
    second_out[:, 768:864] = last[:, 0:96]
    third_out[...] = last[0:6, 96:128]
    first_out[...] = final[14:16].reshape(32, 128)[:, 0:108]
    write.wait()


def on_device(fields, viscosity, samples, trainers, conv_first, conv_second, conv_third):
    vmem = pl.BlockSpec(memory_space=pltpu.VMEM)
    smem = pl.BlockSpec(memory_space=pltpu.SMEM)
    hbm = pl.BlockSpec(memory_space=pl.ANY)
    dma = pltpu.SemaphoreType.DMA
    v = pltpu.VMEM
    advanced, losses, first, second, third = pl.pallas_call(
        whole_kernel,
        out_shape=(
            jax.ShapeDtypeStruct((4, 8, 32, 128), F32),
            jax.ShapeDtypeStruct((1, 32), F32),
            jax.ShapeDtypeStruct((32, 108), F32),
            jax.ShapeDtypeStruct((32, 864), F32),
            jax.ShapeDtypeStruct((6, 32), F32),
        ),
        in_specs=[hbm, hbm, smem, smem, hbm, hbm, hbm],
        out_specs=(hbm, vmem, vmem, vmem, vmem),
        scratch_shapes=[
            v((5, 10, 32, 128), F32), v((4, 10, 32, 128), F32), v((4, 8, 32, 128), F32),
            v((2, 5, 8, 128), F32), v((2, 5, 8, 128), F32),
            v((2, 16, 128), F32), v((2, 16, 128), F32),
            v((2, 4, 8, 128), F32), v((2, 4, 8, 128), F32),
            v((2, 8, 128), F32), v((2, 8, 128), F32),
            v((5, 8, 32, 128), F32),
            v((1, 128), I32), v((16, 1, 128), I32), v((1, 128), F32), v((16, 1, 128), F32),
            v((32, 108), BF16), v((32, 864), BF16), v((6, 32), BF16),
            v((128, 512), F32), v((864, 512), BF16),
            v((16, 16, 128), F32), v((16, 16, 128), F32), v((16, 128), F32),
            v((16, 16, 128), F32), v((16, 128), F32), v((16, 16, 128), F32),
            dma((6,)),
            dma((2,)), dma((2,)), dma((2,)), dma((2,)), dma, dma,
            dma((2,)), dma((2,)), dma((2,)), dma((2,)), dma, dma,
            dma((16,)), dma((16,)), dma((16,)), dma((16,)),
            dma((16,)), dma((16,)), dma((16,)), dma((16,)), dma((16,)), dma((16,)),
        ],
        compiler_params=pltpu.CompilerParams(
            collective_id=0, has_side_effects=True, vmem_limit_bytes=48 * 1024 * 1024
        ),
        name="step",
    )(
        fields, viscosity, samples.reshape(8), trainers.reshape(8),
        conv_first, conv_second, conv_third,
    )
    return advanced, losses.reshape(1, 1, 1, 32), first, second, third


def solution(mesh):
    in_specs = (
        P(None, "gx", "gy", "gz"),
        P("gx", "gy", "gz"),
        P("gx", "gy", "gz", None),
        P("gx", "gy", "gz", None, None),
        P(),
        P(),
        P(),
    )
    out_specs = (P(None, "gx", "gy", "gz"), P("gx", "gy", "gz", None), P(), P(), P())
    return jax.shard_map(
        on_device, mesh=mesh, in_specs=in_specs, out_specs=out_specs, check_vma=False
    )
```

```python
import jax
import jax.numpy as jnp
from jax import lax
from jax.experimental import pallas as pl
from jax.experimental.pallas import tpu as pltpu
from jax.sharding import PartitionSpec as P

MESH = pl.DeviceIdType.MESH
F32 = jnp.float32
BF16 = jnp.bfloat16
I32 = jnp.int32
HIGH = lax.Precision.HIGHEST

NX, NY, NZ = 8, 16, 2
WORKERS = NX * NY * NZ
NT = (((1,), (1,)), ((), ()))
TN = (((0,), (0,)), ((), ()))
TIME_STEP = 0.25
BUOYANCY = 0.5
PAIR_P = (0, 1, 2, 0, 0, 1)
PAIR_Q = (0, 1, 2, 1, 2, 2)


def iota(shape, dim):
    return lax.broadcasted_iota(I32, shape, dim)


def flux(low, high, visc_low, visc_high, d):
    speed = 0.25 * (low[d] + high[d])
    visc = 0.5 * (visc_low + visc_high)
    return [speed * (a + b) - visc * (b - a) for a, b in zip(low, high)]


def advance_plane(src, visc, halo_y, visc_y, halo_z, p):
    rows = iota((32, 128), 0)
    lanes = iota((32, 128), 1)
    q = [src[c, p] for c in range(4)]
    v = visc(p)
    q_before = [src[c, p - 1] for c in range(4)]
    q_after = [src[c, p + 1] for c in range(4)]
    total = [
        a - b
        for a, b in zip(flux(q, q_after, v, visc(p + 1), 0), flux(q_before, q, visc(p - 1), v, 0))
    ]
    at = pl.ds(p - 1, 1)
    y_low = [halo_y[0, c, at] for c in range(4)]
    y_high = [halo_y[1, c, at] for c in range(4)]

    def up(x, edge):
        return jnp.where(rows == 31, edge, pltpu.roll(x, 31, 0))

    q_next = [up(x, e) for x, e in zip(q, y_high)]
    faces = flux(q, q_next, v, up(v, visc_y[1, 4, at]), 1)
    first = flux(y_low, [x[0:1] for x in q], visc_y[0, 4, at], v[0:1], 1)
    total = [
        t + (f - jnp.where(rows == 0, e, pltpu.roll(f, 1, 0)))
        for t, f, e in zip(total, faces, first)
    ]
    side = [halo_z[c, p - 1] for c in range(4)]
    side_v = halo_z[4, p - 1]

    def along(x, edge):
        return jnp.where(lanes == 127, edge, pltpu.roll(x, 127, 1))

    q_next = [along(x, e) for x, e in zip(q, side)]
    faces = flux(q, q_next, v, along(v, side_v), 2)
    first = flux(side, q, side_v, v, 2)
    total = [
        t + (f - jnp.where(lanes == 0, e, pltpu.roll(f, 1, 1)))
        for t, f, e in zip(total, faces, first)
    ]
    out = [x - TIME_STEP * t for x, t in zip(q, total)]
    out[2] = out[2] + (TIME_STEP * BUOYANCY) * q[3]
    return out


def pack_sides(src, count, y_send, z_send):
    for c in range(count):
        y_send[0, c] = src[c, 1:9, 0, :]
        y_send[1, c] = src[c, 1:9, 31, :]
        for h in range(2):
            turned = src[c, 1 + 4 * h : 5 + 4 * h].reshape(128, 128).T
            g = 2 * c + h
            z_send[0, g : g + 1, :] = turned[0:1]
            z_send[1, g : g + 1, :] = turned[127:128]


def unpack_sides(z_recv, count, halo_z):
    rows = iota((128, 128), 0)
    for c in range(count):
        for h in range(2):
            g = 2 * c + h
            first = z_recv[0, g : g + 1, :]
            last = z_recv[1, g : g + 1, :]
            placed = jnp.where(rows == 0, last, jnp.where(rows == 127, first, 0.0))
            halo_z[c, 4 * h : 4 * h + 4] = placed.T.reshape(4, 32, 128)


def by_lane(values, lanes_of):
    out = jnp.zeros(lanes_of.shape, I32)
    for j in range(8):
        out = jnp.where(lanes_of == j, values[j], out)
    return out


def shifts():
    return [(ox, oy) for ox in (-1, 0, 1) for oy in (-1, 0, 1)]


def inside(shape, ox, oy):
    lanes = iota(shape, 1)
    x = lanes // 4 % 4 + ox
    y = lanes % 4 + oy
    return (x >= 0) & (x < 4) & (y >= 0) & (y < 4)


def rolled(x, ox, oy):
    if ox == 0 and oy == 0:
        return x
    moved = pltpu.roll(x, (-(4 * ox + oy)) % 128, 1)
    return jnp.where(inside(x.shape, ox, oy), moved, 0.0)


def box(x):
    rows = iota(x.shape, 0) % 4
    lanes = iota(x.shape, 1)
    count = x.shape[0]
    x = (
        x
        + jnp.where(rows > 0, pltpu.roll(x, 1, 0), 0.0)
        + jnp.where(rows < 3, pltpu.roll(x, count - 1, 0), 0.0)
    )
    for step, place in ((1, lanes % 4), (4, lanes // 4 % 4)):
        x = (
            x
            + jnp.where(place > 0, pltpu.roll(x, step, 1), 0.0)
            + jnp.where(place < 3, pltpu.roll(x, 128 - step, 1), 0.0)
        )
    return x / 27.0


def cat_rows(x):
    return jnp.concatenate([x[:, 128 * z : 128 * z + 128] for z in range(4)], axis=0)


def dot(a, b, dims=None, precision=None):
    if dims is None:
        dims = (((1,), (0,)), ((), ()))
    return lax.dot_general(a, b, dims, precision=precision, preferred_element_type=F32)


def whole_kernel(
    fields_hbm, visc_hbm, samples, trainers, w1_hbm, w2_hbm, w3_hbm,
    adv_hbm, loss_hbm, final,
    start, mid, adv, y_send, y_recv, z_send, z_recv, y_send2, y_recv2, z_send2, z_recv2,
    halo_z, t_send, t_recv, l_send, l_recv, w1, w2, w3, st1, st2,
    grads, part, sum1, spread, sum2, loss_out,
    local_sem, x_s, x_r, y_s, y_r, z_s, z_r, x2_s, x2_r, y2_s, y2_r, z2_s, z2_r,
    t_s, t_r, l_s, l_r, a_s, a_r, b_s, b_r, c_s, c_r,
):
    ax = lax.axis_index("gx")
    ay = lax.axis_index("gy")
    az = lax.axis_index("gz")
    aw = ax * NZ + az

    def in_y(d):
        return (ax, lax.rem(ay + d, NY), az)

    def in_w(d):
        w = lax.rem(aw + d, NX * NZ)
        return (w // NZ, ay, lax.rem(w, NZ))

    loads = [
        pltpu.make_async_copy(fields_hbm, start.at[0:4, 1:9], local_sem.at[0]),
        pltpu.make_async_copy(visc_hbm, start.at[4, 1:9], local_sem.at[1]),
        pltpu.make_async_copy(w1_hbm, w1, local_sem.at[2]),
        pltpu.make_async_copy(w2_hbm, w2, local_sem.at[3]),
        pltpu.make_async_copy(w3_hbm, w3, local_sem.at[4]),
    ]
    for load in loads:
        load.start()

    barrier = pltpu.get_barrier_semaphore()

    def greet(d, carry):
        pl.semaphore_signal(barrier, inc=1, device_id=in_y(d), device_id_type=MESH)
        pl.semaphore_signal(barrier, inc=1, device_id=in_w(d), device_id_type=MESH)
        return carry

    lax.fori_loop(1, 16, greet, 0)
    picked = [samples[j] for j in range(8)]
    owners = [trainers[j] for j in range(8)]
    t_send[...] = by_lane(owners, iota((1, 128), 1) % 8)
    loads[0].wait()
    loads[1].wait()
    pl.semaphore_wait(barrier, 30)

    def remote(src, dst, s, r, to):
        return pltpu.make_async_remote_copy(
            src_ref=src, dst_ref=dst, send_sem=s, recv_sem=r, device_id=to, device_id_type=MESH
        )

    x_up = (lax.rem(ax + 1, NX), ay, az)
    x_down = (lax.rem(ax + NX - 1, NX), ay, az)
    other = (ax, ay, 1 - az)

    def exchange_x(ref, s, r):
        return [
            remote(ref.at[:, 8], ref.at[:, 0], s.at[0], r.at[0], x_up),
            remote(ref.at[:, 1], ref.at[:, 9], s.at[1], r.at[1], x_down),
        ]

    def exchange_yz(ys, yr, zs, zr, ysem, yrem, zsem, zrem):
        return [
            remote(ys.at[1], yr.at[0], ysem.at[0], yrem.at[0], in_y(1)),
            remote(ys.at[0], yr.at[1], ysem.at[1], yrem.at[1], in_y(NY - 1)),
            remote(zs, zr, zsem, zrem, other),
        ]

    moves = exchange_x(start, x_s, x_r)
    for move in moves:
        move.start()
    pack_sides(start, 5, y_send, z_send)
    sides = exchange_yz(y_send, y_recv, z_send, z_recv, y_s, y_r, z_s, z_r)
    for move in sides:
        move.start()

    def everyone(src, buf, s, r, slot, to):
        def begin(d, carry):
            remote(src, buf.at[slot], s.at[d], r.at[slot], to(d)).start()
            return carry

        lax.fori_loop(1, 16, begin, 0)

    def all_here(src, buf, s, r, slot, to):
        def finish(d, carry):
            at = lax.rem(slot + d, 16)
            copy = remote(src, buf.at[at], s.at[d], r.at[at], to(d))
            copy.wait_send()
            copy.wait_recv()
            return carry

        lax.fori_loop(1, 16, finish, 0)

    everyone(t_send, t_recv, t_s, t_r, ay, in_y)
    t_recv[ay] = t_send[...]

    for move in sides:
        move.wait()
    unpack_sides(z_recv, 5, halo_z)
    for move in moves:
        move.wait()

    def visc(p):
        return start[4, p]

    def store_mid(p):
        for c, x in enumerate(advance_plane(start, visc, y_recv, y_recv, halo_z, p)):
            mid[c, p] = x

    store_mid(1)
    store_mid(8)
    moves = exchange_x(mid, x2_s, x2_r)
    for move in moves:
        move.start()

    def first_step(p, carry):
        store_mid(p)
        return carry

    lax.fori_loop(2, 8, first_step, 0)
    pack_sides(mid, 4, y_send2, z_send2)
    sides = exchange_yz(y_send2, y_recv2, z_send2, z_recv2, y2_s, y2_r, z2_s, z2_r)
    for move in sides:
        move.start()
    for move in sides:
        move.wait()
    unpack_sides(z_recv2, 4, halo_z)

    def store_adv(p):
        for c, x in enumerate(advance_plane(mid, visc, y_recv2, y_recv, halo_z, p)):
            adv[c, p - 1] = x

    def second_step(p, carry):
        store_adv(p)
        return carry

    lax.fori_loop(2, 8, second_step, 0)
    for move in moves:
        move.wait()
    store_adv(1)
    store_adv(8)
    write = pltpu.make_async_copy(adv, adv_hbm, local_sem.at[5])
    write.start()

    row = iota((128, 256), 0)
    base = by_lane([(s // 256) * 128 + (s // 32 % 8) * 4 for s in picked], row // 16)
    want = base + row // 4 % 4 * 32 + row % 4
    hot = jnp.where(want == iota((128, 256), 1), 1.0, 0.0).astype(BF16)
    lanes128 = iota((128, 128), 1)
    keep = by_lane([s % 32 for s in picked], iota((128, 128), 0) // 16) == lanes128 // 4
    frow = iota((64, 128), 0)
    flane = iota((64, 128), 1)
    comp = frow % 4
    zrow = frow // 4
    for i, c in enumerate(PAIR_P + PAIR_Q):
        here = (frow >= 16 + 4 * i) & (frow < 20 + 4 * i)
        comp = jnp.where(here, c, comp)
    zrow = jnp.where(frow < 16, zrow, frow % 4)
    cells = jnp.zeros((64, 128), F32)
    for c in range(4):
        plane = adv[c].reshape(256, 128).astype(BF16)
        found = jnp.where(keep, dot(hot, plane), 0.0).astype(BF16)
        fold = jnp.where((comp == c) & (flane % 4 == zrow), 1.0, 0.0).astype(BF16)
        cells = cells + dot(fold, found, NT)

    loads[2].wait()
    loads[3].wait()
    loads[4].wait()
    st1[...] = jnp.zeros_like(st1)
    chosen = cells[0:16]
    for i, (ox, oy) in enumerate(shifts()):
        moved = rolled(chosen, ox, oy)
        for o in range(3):
            k = 3 * i + o
            for z in range(4):
                if 0 <= z + o - 1 < 4:
                    st1[4 * k : 4 * k + 4, 128 * z : 128 * z + 128] = moved[
                        4 * (z + o - 1) : 4 * (z + o - 1) + 4
                    ]
    pre1 = cat_rows(dot(w1[...], st1[0:108, :].astype(BF16)))
    sig1 = jax.nn.sigmoid(pre1)
    slope1 = sig1 * (1.0 + pre1 * (1.0 - sig1))
    hid1 = (pre1 * sig1).astype(BF16).astype(F32)
    for i, (ox, oy) in enumerate(shifts()):
        moved = rolled(hid1, ox, oy).astype(BF16)
        for o in range(3):
            k = 3 * i + o
            for z in range(4):
                if 0 <= z + o - 1 < 4:
                    piece = moved[32 * (z + o - 1) : 32 * (z + o)]
                else:
                    piece = jnp.zeros((32, 128), BF16)
                st2[32 * k : 32 * k + 32, 128 * z : 128 * z + 128] = piece
    pre2 = cat_rows(dot(w2[...], st2[0:864, :]))
    sig2 = jax.nn.sigmoid(pre2)
    slope2 = sig2 * (1.0 + pre2 * (1.0 - sig2))
    hid2 = (pre2 * sig2).astype(BF16)
    pick_row = jnp.where(iota((24, 6), 0) // 4 == iota((24, 6), 1), 1.0, 0.0).astype(BF16)
    pick_col = jnp.where(iota((32, 128), 1) % 32 == iota((32, 128), 0), 1.0, 0.0).astype(BF16)
    spread3 = dot(dot(pick_row, w3[...]).astype(BF16), pick_col)
    same_z = iota((24, 128), 0) % 4 == iota((24, 128), 1) // 32
    wide3 = jnp.where(same_z, spread3, 0.0).astype(BF16)
    predicted = dot(wide3, hid2)
    up_p, up_q = cells[16:40], cells[40:64]
    target = box(up_p * up_q) - box(up_p) * box(up_q)
    misfit = predicted - target

    squares = jnp.broadcast_to(jnp.sum(misfit * misfit, axis=0, keepdims=True), (8, 128))
    group = jnp.where(iota((128, 128), 0) // 16 == lanes128 % 8, 1.0, 0.0)
    l_send[...] = dot(squares, group, precision=HIGH)[0:1] / 384.0
    all_here(t_send, t_recv, t_s, t_r, ay, in_y)
    everyone(l_send, l_recv, l_s, l_r, ay, in_y)
    l_recv[ay] = l_send[...]
    owned = t_recv[:, 0, :]
    mine = by_lane(owners, iota((16, 128), 1) // 16)
    load = jnp.zeros((16, 128), F32)
    for s in range(8):
        other_owner = owned if s == 0 else pltpu.roll(owned, s, 1)
        load = load + jnp.where(other_owner == mine, 1.0, 0.0)
    load = jnp.sum(load, axis=0, keepdims=True)
    share = 1.0 / (WORKERS * jnp.maximum(load, 1.0))
    grad_pred = (misfit * (share * (2.0 / 384.0))).astype(BF16)

    third = jnp.where(same_z, dot(grad_pred, hid2, NT), 0.0)
    third = jnp.concatenate(
        [jnp.sum(third[4 * i : 4 * i + 4], axis=0, keepdims=True) for i in range(6)]
        + [jnp.zeros((26, 128), F32)],
        axis=0,
    )
    third = third + pltpu.roll(third, 32, 1)
    third = third + pltpu.roll(third, 64, 1)
    grad_mid = (dot(wide3, grad_pred, TN) * slope2).astype(BF16)
    mid_cols = jnp.concatenate([grad_mid[32 * z : 32 * z + 32] for z in range(4)], axis=1)

    def send_tile(i):
        for h in range(2):
            to = 2 * i + h

            @pl.when(aw != to)
            def _():
                remote(
                    grads.at[to], part.at[aw], a_s.at[to], a_r.at[aw], (to // NZ, ay, to % NZ)
                ).start()

    def store_tile(i, x):
        grads[2 * i] = x[0:16]
        grads[2 * i + 1] = x[16:32]

    for i in range(7):
        rows_here = 128 if i < 6 else 96
        tile = dot(mid_cols, st2[128 * i : 128 * i + rows_here, :], NT)
        if i == 6:
            tile = jnp.concatenate([tile, third[:, 96:128]], axis=1)
        store_tile(i, tile)
        send_tile(i)
    lower = jnp.zeros((128, 128), F32)
    for i, (ox, oy) in enumerate(shifts()):
        y = dot(w2[:, 96 * i : 96 * i + 96], mid_cols, TN)
        parts = []
        for z in range(4):
            total = y[32:64, 128 * z : 128 * z + 128]
            if z + 1 < 4:
                total = total + y[0:32, 128 * z + 128 : 128 * z + 256]
            if z - 1 >= 0:
                total = total + y[64:96, 128 * z - 128 : 128 * z]
            parts.append(total)
        lower = lower + rolled(jnp.concatenate(parts, axis=0), -ox, -oy)
    entry = (lower * slope1).astype(BF16)
    entry_cols = jnp.concatenate([entry[32 * z : 32 * z + 32] for z in range(4)], axis=1)
    store_tile(7, dot(entry_cols, st1[...].astype(BF16), NT))
    send_tile(7)

    part[aw] = grads[aw]
    for to in range(16):

        @pl.when(aw != to)
        def _():
            remote(
                grads.at[to], part.at[to], a_s.at[to], a_r.at[to], (to // NZ, ay, to % NZ)
            ).wait()

    def added(buf):
        total = buf[0]
        for s in range(1, 16):
            total = total + buf[s]
        return total

    sum1[...] = added(part)
    everyone(sum1, spread, b_s, b_r, ay, in_y)
    spread[ay] = sum1[...]

    all_here(l_send, l_recv, l_s, l_r, ay, in_y)
    lanes16 = iota((16, 128), 1)
    rank = jnp.zeros((16, 128), I32)
    for s in range(1, 8):
        earlier = (pltpu.roll(owned, s, 1) == owned) & (lanes16 % 8 >= s)
        rank = rank + jnp.where(earlier, 1, 0)
    losses = l_recv[:, 0, :]
    own = (owned == ay) & (lanes16 < 8)
    place = lanes16 - 2 * iota((16, 128), 0)
    slots = jnp.zeros((16, 128), F32)
    for r in range(2):
        value = jnp.sum(jnp.where(own & (rank == r), losses, 0.0), axis=1, keepdims=True)
        slots = slots + jnp.where(place == r, value, 0.0)
    loss_out[...] = jnp.sum(slots, axis=0, keepdims=True)[:, 0:32]
    write_loss = pltpu.make_async_copy(loss_out, loss_hbm, local_sem.at[6])
    write_loss.start()

    all_here(sum1, spread, b_s, b_r, ay, in_y)
    sum2[...] = added(spread)
    everyone(sum2, final, c_s, c_r, aw, in_w)
    own_part = pltpu.make_async_copy(sum2, final.at[aw], local_sem.at[7])
    own_part.start()
    write.wait()
    write_loss.wait()
    own_part.wait()
    all_here(sum2, final, c_s, c_r, aw, in_w)


def hand_over_kernel(
    adv_in, loss_in, final_in, adv_out, loss_out, first_out, second_out, third_out,
    adv, loss, final, first, second, third, sem,
):
    loads = [pltpu.make_async_copy(adv_in.at[c], adv.at[c], sem.at[c]) for c in range(4)]
    loads.append(pltpu.make_async_copy(loss_in, loss, sem.at[4]))
    load_final = pltpu.make_async_copy(final_in, final, sem.at[5])
    load_final.start()
    for load in loads:
        load.start()
    load_final.wait()
    for i in range(6):
        second[:, 128 * i : 128 * i + 128] = final[2 * i : 2 * i + 2].reshape(32, 128)
    last = final[12:14].reshape(32, 128)
    second[:, 768:864] = last[:, 0:96]
    third[...] = last[0:6, 96:128]
    first[...] = final[14:16].reshape(32, 128)[:, 0:108]
    stores = [
        pltpu.make_async_copy(second, second_out, sem.at[6]),
        pltpu.make_async_copy(first, first_out, sem.at[7]),
        pltpu.make_async_copy(third, third_out, sem.at[8]),
    ]
    for store in stores:
        store.start()
    for c in range(4):
        loads[c].wait()
        stores.append(pltpu.make_async_copy(adv.at[c], adv_out.at[c], sem.at[9 + c]))
        stores[-1].start()
    loads[4].wait()
    stores.append(pltpu.make_async_copy(loss, loss_out, sem.at[13]))
    stores[-1].start()
    for store in stores:
        store.wait()


def on_device(fields, viscosity, samples, trainers, conv_first, conv_second, conv_third):
    smem = pl.BlockSpec(memory_space=pltpu.SMEM)
    hbm = pl.BlockSpec(memory_space=pl.ANY)
    dma = pltpu.SemaphoreType.DMA
    v = pltpu.VMEM
    shapes = (
        jax.ShapeDtypeStruct((4, 8, 32, 128), F32),
        jax.ShapeDtypeStruct((1, 32), F32),
        jax.ShapeDtypeStruct((32, 108), F32),
        jax.ShapeDtypeStruct((32, 864), F32),
        jax.ShapeDtypeStruct((6, 32), F32),
    )
    results = pl.pallas_call(
        whole_kernel,
        out_shape=(shapes[0], shapes[1], jax.ShapeDtypeStruct((16, 16, 128), F32)),
        in_specs=[hbm, hbm, smem, smem, hbm, hbm, hbm],
        out_specs=(hbm,) * 3,
        scratch_shapes=[
            v((5, 10, 32, 128), F32), v((4, 10, 32, 128), F32), v((4, 8, 32, 128), F32),
            v((2, 5, 8, 128), F32), v((2, 5, 8, 128), F32),
            v((2, 16, 128), F32), v((2, 16, 128), F32),
            v((2, 4, 8, 128), F32), v((2, 4, 8, 128), F32),
            v((2, 8, 128), F32), v((2, 8, 128), F32),
            v((5, 8, 32, 128), F32),
            v((1, 128), I32), v((16, 1, 128), I32), v((1, 128), F32), v((16, 1, 128), F32),
            v((32, 108), BF16), v((32, 864), BF16), v((6, 32), BF16),
            v((128, 512), F32), v((864, 512), BF16),
            v((16, 16, 128), F32), v((16, 16, 128), F32), v((16, 128), F32),
            v((16, 16, 128), F32), v((16, 128), F32), v((1, 32), F32),
            dma((8,)),
            dma((2,)), dma((2,)), dma((2,)), dma((2,)), dma, dma,
            dma((2,)), dma((2,)), dma((2,)), dma((2,)), dma, dma,
            dma((16,)), dma((16,)), dma((16,)), dma((16,)),
            dma((16,)), dma((16,)), dma((16,)), dma((16,)), dma((16,)), dma((16,)),
        ],
        compiler_params=pltpu.CompilerParams(
            collective_id=0, has_side_effects=True, vmem_limit_bytes=60 * 1024 * 1024
        ),
        name="step",
    )(
        fields, viscosity, samples.reshape(8), trainers.reshape(8),
        conv_first, conv_second, conv_third,
    )
    advanced, losses, first, second, third = pl.pallas_call(
        hand_over_kernel,
        out_shape=shapes,
        in_specs=[hbm] * 3,
        out_specs=(hbm,) * 5,
        scratch_shapes=[
            v((4, 8, 32, 128), F32), v((1, 32), F32), v((16, 16, 128), F32),
            v((32, 108), F32), v((32, 864), F32), v((6, 32), F32), dma((14,)),
        ],
        compiler_params=pltpu.CompilerParams(vmem_limit_bytes=60 * 1024 * 1024),
        name="hand_over",
    )(*results)
    return advanced, losses.reshape(1, 1, 1, 32), first, second, third


def solution(mesh):
    in_specs = (
        P(None, "gx", "gy", "gz"),
        P("gx", "gy", "gz"),
        P("gx", "gy", "gz", None),
        P("gx", "gy", "gz", None, None),
        P(),
        P(),
        P(),
    )
    out_specs = (P(None, "gx", "gy", "gz"), P("gx", "gy", "gz", None), P(), P(), P())
    return jax.shard_map(
        on_device, mesh=mesh, in_specs=in_specs, out_specs=out_specs, check_vma=False
    )
```

```python
import jax
import jax.numpy as jnp
from jax import lax
from jax.experimental import pallas as pl
from jax.experimental.pallas import tpu as pltpu
from jax.sharding import PartitionSpec as P

MESH = pl.DeviceIdType.MESH
F32 = jnp.float32
BF16 = jnp.bfloat16
I32 = jnp.int32
HIGH = lax.Precision.HIGHEST

NX, NY, NZ = 8, 16, 2
WORKERS = NX * NY * NZ
NT = (((1,), (1,)), ((), ()))
TN = (((0,), (0,)), ((), ()))
TIME_STEP = 0.25
BUOYANCY = 0.5
PAIR_P = (0, 1, 2, 0, 0, 1)
PAIR_Q = (0, 1, 2, 1, 2, 2)


def iota(shape, dim):
    return lax.broadcasted_iota(I32, shape, dim)


def flux(low, high, visc_low, visc_high, d):
    speed = 0.25 * (low[d] + high[d])
    visc = 0.5 * (visc_low + visc_high)
    return [speed * (a + b) - visc * (b - a) for a, b in zip(low, high)]


def inner_part(src, visc, store):
    rows = iota((32, 128), 0)
    lanes = iota((32, 128), 1)

    def plane(p, before, is_last):
        q = [src[c, p] for c in range(4)]
        v = visc(p)
        if is_last:
            after = None
            total = [-b for b in before]
        else:
            after = flux(q, [src[c, p + 1] for c in range(4)], v, visc(p + 1), 0)
            total = after if before is None else [a - b for a, b in zip(after, before)]
        for axis, size, edge, d in ((0, 32, rows == 31, 1), (1, 128, lanes == 127, 2)):
            q_next = [pltpu.roll(x, size - 1, axis) for x in q]
            faces = flux(q, q_next, v, pltpu.roll(v, size - 1, axis), d)
            faces = [jnp.where(edge, 0.0, f) for f in faces]
            total = [t + (f - pltpu.roll(f, 1, axis)) for t, f in zip(total, faces)]
        out = [x - TIME_STEP * t for x, t in zip(q, total)]
        out[2] = out[2] + (TIME_STEP * BUOYANCY) * q[3]
        store(p, out)
        return after

    def body(p, before):
        return tuple(plane(p, before, False))

    before = lax.fori_loop(2, 8, body, tuple(plane(1, None, False)))
    plane(8, before, True)


def edge_part(src, visc, dst, first, y_own, y_far, y_visc, z_own, z_far, z_visc):
    rows = iota((128, 128), 0)
    own_low = [z_own[0, 2 * c : 2 * c + 2] for c in range(4)]
    own_high = [z_own[1, 2 * c : 2 * c + 2] for c in range(4)]
    far_low = [z_far[0, 2 * c : 2 * c + 2] for c in range(4)]
    far_high = [z_far[1, 2 * c : 2 * c + 2] for c in range(4)]
    (v_own, v_far) = z_visc
    low = flux(far_high, own_low, v_far[1, 8:10], v_own[0, 8:10], 2)
    high = flux(own_high, far_low, v_own[1, 8:10], v_far[0, 8:10], 2)
    for c in range(4):
        for h in range(2):
            placed = jnp.where(
                rows == 0,
                TIME_STEP * low[c][h : h + 1],
                jnp.where(rows == 127, -TIME_STEP * high[c][h : h + 1], 0.0),
            )
            planes = slice(first + 4 * h, first + 4 * h + 4)
            dst[c, planes] = dst[c, planes] + placed.T.reshape(4, 32, 128)
    (v_own, v_far) = y_visc

    def face(ref, side):
        return [ref[side, c] for c in range(4)]

    low = flux(face(y_far, 0), face(y_own, 0), v_far[0, 4], v_own[0, 4], 1)
    high = flux(face(y_own, 1), face(y_far, 1), v_own[1, 4], v_far[1, 4], 1)
    planes = slice(first, first + 8)
    for c in range(4):
        dst[c, planes, 0, :] = dst[c, planes, 0, :] + TIME_STEP * low[c]
        dst[c, planes, 31, :] = dst[c, planes, 31, :] - TIME_STEP * high[c]

    def of(p):
        return [src[c, p] for c in range(4)]

    low = flux(of(0), of(1), visc(0), visc(1), 0)
    high = flux(of(8), of(9), visc(8), visc(9), 0)
    for c in range(4):
        dst[c, first] = dst[c, first] + TIME_STEP * low[c]
        dst[c, first + 7] = dst[c, first + 7] - TIME_STEP * high[c]


def pack_sides(src, count, y_send, z_send):
    for c in range(count):
        y_send[0, c] = src[c, 1:9, 0, :]
        y_send[1, c] = src[c, 1:9, 31, :]
        for h in range(2):
            turned = src[c, 1 + 4 * h : 5 + 4 * h].reshape(128, 128).T
            g = 2 * c + h
            z_send[0, g : g + 1, :] = turned[0:1]
            z_send[1, g : g + 1, :] = turned[127:128]


def by_lane(values, lanes_of):
    out = jnp.zeros(lanes_of.shape, I32)
    for j in range(8):
        out = jnp.where(lanes_of == j, values[j], out)
    return out


def shifts():
    return [(ox, oy) for ox in (-1, 0, 1) for oy in (-1, 0, 1)]


def inside(ox, oy):
    lanes = iota((1, 128), 1)
    x = lanes // 4 % 4 + ox
    y = lanes % 4 + oy
    return jnp.where((x >= 0) & (x < 4) & (y >= 0) & (y < 4), 1.0, 0.0)


def rolled(x, ox, oy):
    if ox == 0 and oy == 0:
        return x
    return pltpu.roll(x, (-(4 * ox + oy)) % 128, 1) * inside(ox, oy)


def box(x):
    rows = iota(x.shape, 0) % 4
    lanes = iota(x.shape, 1)
    count = x.shape[0]
    x = (
        x
        + jnp.where(rows > 0, pltpu.roll(x, 1, 0), 0.0)
        + jnp.where(rows < 3, pltpu.roll(x, count - 1, 0), 0.0)
    )
    for step, place in ((1, lanes % 4), (4, lanes // 4 % 4)):
        x = (
            x
            + jnp.where(place > 0, pltpu.roll(x, step, 1), 0.0)
            + jnp.where(place < 3, pltpu.roll(x, 128 - step, 1), 0.0)
        )
    return x / 27.0


def cat_rows(x):
    return jnp.concatenate([x[:, 128 * z : 128 * z + 128] for z in range(4)], axis=0)


def dot(a, b, dims=None, precision=None):
    if dims is None:
        dims = (((1,), (0,)), ((), ()))
    return lax.dot_general(a, b, dims, precision=precision, preferred_element_type=F32)


def whole_kernel(
    fields_hbm, visc_hbm, samples_hbm, trainers_hbm, w1_hbm, w2_hbm, w3_hbm,
    adv_hbm, loss_hbm, final,
    samples, trainers,
    start, mid, adv, y_send, y_recv, z_send, z_recv, y_send2, y_recv2, z_send2, z_recv2,
    t_send, t_recv, l_send, l_recv, w1, w2, w3, w2_turned, hot, keep, folds, st1, st2,
    grads, part, sum1, spread, sum2, loss_out,
    local_sem, x_s, x_r, y_s, y_r, z_s, z_r, x2_s, x2_r, y2_s, y2_r, z2_s, z2_r,
    t_s, t_r, l_s, l_r, a_s, a_r, b_s, b_r, c_s, c_r,
):
    ax = lax.axis_index("gx")
    ay = lax.axis_index("gy")
    az = lax.axis_index("gz")
    aw = ax * NZ + az

    def in_y(d):
        return (ax, lax.rem(ay + d, NY), az)

    def in_w(d):
        w = lax.rem(aw + d, NX * NZ)
        return (w // NZ, ay, lax.rem(w, NZ))

    loads = [
        pltpu.make_async_copy(src, dst, local_sem.at[i])
        for i, (src, dst) in enumerate(
            (
                (fields_hbm, start.at[0:4, 1:9]),
                (visc_hbm, start.at[4, 1:9]),
                (trainers_hbm, trainers),
                (samples_hbm, samples),
                (w1_hbm, w1),
                (w2_hbm, w2),
                (w3_hbm, w3),
            )
        )
    ]
    loads[0].start()
    loads[1].start()
    barrier = pltpu.get_barrier_semaphore()

    def greet(d, carry):
        pl.semaphore_signal(barrier, inc=1, device_id=in_y(d), device_id_type=MESH)
        pl.semaphore_signal(barrier, inc=1, device_id=in_w(d), device_id_type=MESH)
        return carry

    lax.fori_loop(1, 16, greet, 0)
    for load in loads[2:]:
        load.start()
    loads[0].wait()
    loads[1].wait()
    pack_sides(start, 5, y_send, z_send)
    loads[2].wait()
    owners = [trainers[j] for j in range(8)]
    t_send[...] = by_lane(owners, iota((1, 128), 1) % 8)
    pl.semaphore_wait(barrier, 30)

    def remote(src, dst, s, r, to):
        return pltpu.make_async_remote_copy(
            src_ref=src, dst_ref=dst, send_sem=s, recv_sem=r, device_id=to, device_id_type=MESH
        )

    x_up = (lax.rem(ax + 1, NX), ay, az)
    x_down = (lax.rem(ax + NX - 1, NX), ay, az)
    other = (ax, ay, 1 - az)

    def exchange_x(ref, s, r):
        return [
            remote(ref.at[:, 8], ref.at[:, 0], s.at[0], r.at[0], x_up),
            remote(ref.at[:, 1], ref.at[:, 9], s.at[1], r.at[1], x_down),
        ]

    def exchange_yz(ys, yr, zs, zr, ysem, yrem, zsem, zrem):
        return [
            remote(ys.at[1], yr.at[0], ysem.at[0], yrem.at[0], in_y(1)),
            remote(ys.at[0], yr.at[1], ysem.at[1], yrem.at[1], in_y(NY - 1)),
            remote(zs, zr, zsem, zrem, other),
        ]

    def everyone(src, buf, s, r, slot, to):
        def begin(d, carry):
            remote(src, buf.at[slot], s.at[d], r.at[slot], to(d)).start()
            return carry

        lax.fori_loop(1, 16, begin, 0)

    def all_here(src, buf, s, r, slot, to):
        def finish(d, carry):
            at = lax.rem(slot + d, 16)
            copy = remote(src, buf.at[at], s.at[d], r.at[at], to(d))
            copy.wait_send()
            copy.wait_recv()
            return carry

        lax.fori_loop(1, 16, finish, 0)

    moves = exchange_x(start, x_s, x_r)
    moves += exchange_yz(y_send, y_recv, z_send, z_recv, y_s, y_r, z_s, z_r)
    for move in moves:
        move.start()
    everyone(t_send, t_recv, t_s, t_r, ay, in_y)
    t_recv[ay] = t_send[...]

    def visc(p):
        return start[4, p]

    def store_mid(p, out):
        for c in range(4):
            mid[c, p] = out[c]

    inner_part(start, visc, store_mid)
    loads[3].wait()
    picked = [samples[j] for j in range(8)]
    row = iota((128, 256), 0)
    base = by_lane([(s // 256) * 128 + (s // 32 % 8) * 4 for s in picked], row // 16)
    want = base + row // 4 % 4 * 32 + row % 4
    hot[...] = jnp.where(want == iota((128, 256), 1), 1.0, 0.0).astype(BF16)
    lanes128 = iota((128, 128), 1)
    lz = by_lane([s % 32 for s in picked], iota((128, 128), 0) // 16)
    keep[...] = jnp.where(lz == lanes128 // 4, 1.0, 0.0)
    for move in moves:
        move.wait()
    edge_part(
        start, visc, mid, 1, y_send, y_recv, (y_send, y_recv), z_send, z_recv, (z_send, z_recv)
    )

    moves = exchange_x(mid, x2_s, x2_r)
    for move in moves:
        move.start()
    pack_sides(mid, 4, y_send2, z_send2)
    sides = exchange_yz(y_send2, y_recv2, z_send2, z_recv2, y2_s, y2_r, z2_s, z2_r)
    for move in sides:
        move.start()

    def store_adv(p, out):
        for c in range(4):
            adv[c, p - 1] = out[c]

    inner_part(mid, visc, store_adv)
    frow = iota((64, 128), 0)
    flane = iota((64, 128), 1)
    comp = frow % 4
    for i, c in enumerate(PAIR_P + PAIR_Q):
        here = (frow >= 16 + 4 * i) & (frow < 20 + 4 * i)
        comp = jnp.where(here, c, comp)
    zrow = jnp.where(frow < 16, frow // 4, frow % 4)
    for c in range(4):
        folds[c] = jnp.where((comp == c) & (flane % 4 == zrow), 1.0, 0.0).astype(BF16)
    for load in loads[4:]:
        load.wait()
    st1[...] = jnp.zeros_like(st1)
    st2[...] = jnp.zeros_like(st2)
    for t in range(7):
        width = 128 if t < 6 else 96
        turned = w2[:, 128 * t : 128 * t + width].astype(F32).T
        w2_turned[128 * t : 128 * t + width, :] = turned.astype(BF16)
    pick_row = jnp.where(iota((24, 6), 0) // 4 == iota((24, 6), 1), 1.0, 0.0).astype(BF16)
    pick_col = jnp.where(iota((32, 128), 1) % 32 == iota((32, 128), 0), 1.0, 0.0).astype(BF16)
    spread3 = dot(dot(pick_row, w3[...]).astype(BF16), pick_col)
    same_z = iota((24, 128), 0) % 4 == iota((24, 128), 1) // 32
    wide3 = jnp.where(same_z, spread3, 0.0).astype(BF16)
    all_here(t_send, t_recv, t_s, t_r, ay, in_y)
    owned = t_recv[:, 0, :]
    mine = by_lane(owners, iota((16, 128), 1) // 16)
    load = jnp.zeros((16, 128), F32)
    for s in range(8):
        other_owner = owned if s == 0 else pltpu.roll(owned, s, 1)
        load = load + jnp.where(other_owner == mine, 1.0, 0.0)
    load = jnp.sum(load, axis=0, keepdims=True)
    share = 1.0 / (WORKERS * jnp.maximum(load, 1.0))
    scale = share * (2.0 / 384.0)
    for move in moves:
        move.wait()
    for move in sides:
        move.wait()
    edge_part(
        mid, visc, adv, 0, y_send2, y_recv2, (y_send, y_recv), z_send2, z_recv2, (z_send, z_recv)
    )
    write = pltpu.make_async_copy(adv, adv_hbm, local_sem.at[7])
    write.start()

    cells = jnp.zeros((64, 128), F32)
    for c in range(4):
        plane = adv[c].reshape(256, 128).astype(BF16)
        found = (dot(hot[...], plane) * keep[...]).astype(BF16)
        cells = cells + dot(folds[c], found, NT)

    chosen = cells[0:16]
    for i, (ox, oy) in enumerate(shifts()):
        moved = rolled(chosen, ox, oy)
        for o in range(3):
            k = 3 * i + o
            for z in range(4):
                if 0 <= z + o - 1 < 4:
                    st1[4 * k : 4 * k + 4, 128 * z : 128 * z + 128] = moved[
                        4 * (z + o - 1) : 4 * (z + o - 1) + 4
                    ]
    pre1 = cat_rows(dot(w1[...], st1[0:108, :].astype(BF16)))
    sig1 = jax.nn.sigmoid(pre1)
    slope1 = sig1 * (1.0 + pre1 * (1.0 - sig1))
    hid1 = (pre1 * sig1).astype(BF16).astype(F32)
    for i, (ox, oy) in enumerate(shifts()):
        moved = rolled(hid1, ox, oy).astype(BF16)
        for o in range(3):
            k = 3 * i + o
            for z in range(4):
                if 0 <= z + o - 1 < 4:
                    st2[32 * k : 32 * k + 32, 128 * z : 128 * z + 128] = moved[
                        32 * (z + o - 1) : 32 * (z + o)
                    ]
    pre2 = cat_rows(dot(w2[...], st2[0:864, :]))
    sig2 = jax.nn.sigmoid(pre2)
    slope2 = sig2 * (1.0 + pre2 * (1.0 - sig2))
    hid2 = (pre2 * sig2).astype(BF16)
    predicted = dot(wide3, hid2)
    up_p, up_q = cells[16:40], cells[40:64]
    smooth = box(jnp.concatenate([up_p * up_q, up_p, up_q], axis=0))
    misfit = predicted - (smooth[0:24] - smooth[24:48] * smooth[48:72])
    grad_pred = (misfit * scale).astype(BF16)

    third = jnp.where(same_z, dot(grad_pred, hid2, NT), 0.0)
    third = jnp.concatenate(
        [jnp.sum(third[4 * i : 4 * i + 4], axis=0, keepdims=True) for i in range(6)]
        + [jnp.zeros((26, 128), F32)],
        axis=0,
    )
    third = third + pltpu.roll(third, 32, 1)
    third = third + pltpu.roll(third, 64, 1)
    grad_mid = (dot(wide3, grad_pred, TN) * slope2).astype(BF16)
    mid_cols = jnp.concatenate([grad_mid[32 * z : 32 * z + 32] for z in range(4)], axis=1)

    def send_tile(i):
        for h in range(2):
            to = 2 * i + h

            @pl.when(aw != to)
            def _():
                remote(
                    grads.at[to], part.at[aw], a_s.at[to], a_r.at[aw], (to // NZ, ay, to % NZ)
                ).start()

    def store_tile(i, x):
        grads[2 * i] = x[0:16]
        grads[2 * i + 1] = x[16:32]

    for i in range(7):
        rows_here = 128 if i < 6 else 96
        tile = dot(mid_cols, st2[128 * i : 128 * i + rows_here, :], NT)
        if i == 6:
            tile = jnp.concatenate([tile, third[:, 96:128]], axis=1)
        store_tile(i, tile)
        send_tile(i)
    lower = jnp.zeros((128, 128), F32)
    for i, (ox, oy) in enumerate(shifts()):
        y = dot(w2_turned[96 * i : 96 * i + 96, :], mid_cols)
        parts = []
        for z in range(4):
            total = y[32:64, 128 * z : 128 * z + 128]
            if z + 1 < 4:
                total = total + y[0:32, 128 * z + 128 : 128 * z + 256]
            if z - 1 >= 0:
                total = total + y[64:96, 128 * z - 128 : 128 * z]
            parts.append(total)
        lower = lower + rolled(jnp.concatenate(parts, axis=0), -ox, -oy)
    entry = (lower * slope1).astype(BF16)
    entry_cols = jnp.concatenate([entry[32 * z : 32 * z + 32] for z in range(4)], axis=1)
    store_tile(7, dot(entry_cols, st1[...].astype(BF16), NT))
    send_tile(7)

    squares = jnp.broadcast_to(jnp.sum(misfit * misfit, axis=0, keepdims=True), (8, 128))
    group = jnp.where(iota((128, 128), 0) // 16 == lanes128 % 8, 1.0, 0.0)
    l_send[...] = dot(squares, group, precision=HIGH)[0:1] / 384.0
    everyone(l_send, l_recv, l_s, l_r, ay, in_y)
    l_recv[ay] = l_send[...]

    part[aw] = grads[aw]
    for to in range(16):

        @pl.when(aw != to)
        def _():
            remote(
                grads.at[to], part.at[to], a_s.at[to], a_r.at[to], (to // NZ, ay, to % NZ)
            ).wait()

    def added(buf):
        total = buf[0]
        for s in range(1, 16):
            total = total + buf[s]
        return total

    sum1[...] = added(part)
    everyone(sum1, spread, b_s, b_r, ay, in_y)
    spread[ay] = sum1[...]

    all_here(l_send, l_recv, l_s, l_r, ay, in_y)
    lanes16 = iota((16, 128), 1)
    rank = jnp.zeros((16, 128), I32)
    for s in range(1, 8):
        earlier = (pltpu.roll(owned, s, 1) == owned) & (lanes16 % 8 >= s)
        rank = rank + jnp.where(earlier, 1, 0)
    losses = l_recv[:, 0, :]
    own = (owned == ay) & (lanes16 < 8)
    place = lanes16 - 2 * iota((16, 128), 0)
    slots = jnp.zeros((16, 128), F32)
    for r in range(2):
        value = jnp.sum(jnp.where(own & (rank == r), losses, 0.0), axis=1, keepdims=True)
        slots = slots + jnp.where(place == r, value, 0.0)
    loss_out[...] = jnp.sum(slots, axis=0, keepdims=True)[:, 0:32]
    write_loss = pltpu.make_async_copy(loss_out, loss_hbm, local_sem.at[8])
    write_loss.start()

    all_here(sum1, spread, b_s, b_r, ay, in_y)
    sum2[...] = added(spread)
    everyone(sum2, final, c_s, c_r, aw, in_w)
    own_part = pltpu.make_async_copy(sum2, final.at[aw], local_sem.at[9])
    own_part.start()
    write.wait()
    write_loss.wait()
    own_part.wait()
    all_here(sum2, final, c_s, c_r, aw, in_w)


def hand_over_kernel(
    adv_in, loss_in, final_in, adv_out, loss_out, first_out, second_out, third_out,
    adv, loss, final, first, second, third, sem,
):
    loads = [pltpu.make_async_copy(adv_in.at[c], adv.at[c], sem.at[c]) for c in range(4)]
    loads.append(pltpu.make_async_copy(loss_in, loss, sem.at[4]))
    load_final = pltpu.make_async_copy(final_in, final, sem.at[5])
    load_final.start()
    for load in loads:
        load.start()
    load_final.wait()
    for i in range(6):
        second[:, 128 * i : 128 * i + 128] = final[2 * i : 2 * i + 2].reshape(32, 128)
    last = final[12:14].reshape(32, 128)
    second[:, 768:864] = last[:, 0:96]
    third[...] = last[0:6, 96:128]
    first[...] = final[14:16].reshape(32, 128)[:, 0:108]
    stores = [
        pltpu.make_async_copy(second, second_out, sem.at[6]),
        pltpu.make_async_copy(first, first_out, sem.at[7]),
        pltpu.make_async_copy(third, third_out, sem.at[8]),
    ]
    for store in stores:
        store.start()
    for c in range(4):
        loads[c].wait()
        stores.append(pltpu.make_async_copy(adv.at[c], adv_out.at[c], sem.at[9 + c]))
        stores[-1].start()
    loads[4].wait()
    stores.append(pltpu.make_async_copy(loss, loss_out, sem.at[13]))
    stores[-1].start()
    for store in stores:
        store.wait()


def on_device(fields, viscosity, samples, trainers, conv_first, conv_second, conv_third):
    hbm = pl.BlockSpec(memory_space=pl.ANY)
    dma = pltpu.SemaphoreType.DMA
    v = pltpu.VMEM
    shapes = (
        jax.ShapeDtypeStruct((4, 8, 32, 128), F32),
        jax.ShapeDtypeStruct((1, 32), F32),
        jax.ShapeDtypeStruct((32, 108), F32),
        jax.ShapeDtypeStruct((32, 864), F32),
        jax.ShapeDtypeStruct((6, 32), F32),
    )
    results = pl.pallas_call(
        whole_kernel,
        out_shape=(shapes[0], shapes[1], jax.ShapeDtypeStruct((16, 16, 128), F32)),
        in_specs=[hbm] * 7,
        out_specs=(hbm,) * 3,
        scratch_shapes=[
            pltpu.SMEM((8,), I32), pltpu.SMEM((8,), I32),
            v((5, 10, 32, 128), F32), v((4, 10, 32, 128), F32), v((4, 8, 32, 128), F32),
            v((2, 5, 8, 128), F32), v((2, 5, 8, 128), F32),
            v((2, 16, 128), F32), v((2, 16, 128), F32),
            v((2, 4, 8, 128), F32), v((2, 4, 8, 128), F32),
            v((2, 8, 128), F32), v((2, 8, 128), F32),
            v((1, 128), I32), v((16, 1, 128), I32), v((1, 128), F32), v((16, 1, 128), F32),
            v((32, 108), BF16), v((32, 864), BF16), v((6, 32), BF16),
            v((864, 32), BF16), v((128, 256), BF16), v((128, 128), F32), v((4, 64, 128), BF16),
            v((128, 512), F32), v((864, 512), BF16),
            v((16, 16, 128), F32), v((16, 16, 128), F32), v((16, 128), F32),
            v((16, 16, 128), F32), v((16, 128), F32), v((1, 32), F32),
            dma((10,)),
            dma((2,)), dma((2,)), dma((2,)), dma((2,)), dma, dma,
            dma((2,)), dma((2,)), dma((2,)), dma((2,)), dma, dma,
            dma((16,)), dma((16,)), dma((16,)), dma((16,)),
            dma((16,)), dma((16,)), dma((16,)), dma((16,)), dma((16,)), dma((16,)),
        ],
        compiler_params=pltpu.CompilerParams(
            collective_id=0, has_side_effects=True, vmem_limit_bytes=60 * 1024 * 1024
        ),
        name="step",
    )(
        fields, viscosity, samples.reshape(8), trainers.reshape(8),
        conv_first, conv_second, conv_third,
    )
    advanced, losses, first, second, third = pl.pallas_call(
        hand_over_kernel,
        out_shape=shapes,
        in_specs=[hbm] * 3,
        out_specs=(hbm,) * 5,
        scratch_shapes=[
            v((4, 8, 32, 128), F32), v((1, 32), F32), v((16, 16, 128), F32),
            v((32, 108), F32), v((32, 864), F32), v((6, 32), F32), dma((14,)),
        ],
        compiler_params=pltpu.CompilerParams(vmem_limit_bytes=60 * 1024 * 1024),
        name="hand_over",
    )(*results)
    return advanced, losses.reshape(1, 1, 1, 32), first, second, third


def solution(mesh):
    in_specs = (
        P(None, "gx", "gy", "gz"),
        P("gx", "gy", "gz"),
        P("gx", "gy", "gz", None),
        P("gx", "gy", "gz", None, None),
        P(),
        P(),
        P(),
    )
    out_specs = (P(None, "gx", "gy", "gz"), P("gx", "gy", "gz", None), P(), P(), P())
    return jax.shard_map(
        on_device, mesh=mesh, in_specs=in_specs, out_specs=out_specs, check_vma=False
    )
```

```python
import jax
import jax.numpy as jnp
from jax import lax
from jax.experimental import pallas as pl
from jax.experimental.pallas import tpu as pltpu
from jax.sharding import PartitionSpec as P

MESH = pl.DeviceIdType.MESH
F32 = jnp.float32
BF16 = jnp.bfloat16
I32 = jnp.int32
HIGH = lax.Precision.HIGHEST

NX, NY, NZ = 8, 16, 2
WORKERS = NX * NY * NZ
NT = (((1,), (1,)), ((), ()))
TN = (((0,), (0,)), ((), ()))
TIME_STEP = 0.25
BUOYANCY = 0.5
PAIR_P = (0, 1, 2, 0, 0, 1)
PAIR_Q = (0, 1, 2, 1, 2, 2)


def iota(shape, dim):
    return lax.broadcasted_iota(I32, shape, dim)


def flux(low, high, visc_low, visc_high, d):
    speed = 0.25 * (low[d] + high[d])
    visc = 0.5 * (visc_low + visc_high)
    return [speed * (a + b) - visc * (b - a) for a, b in zip(low, high)]


def inner_part(src, visc, store):
    rows = iota((32, 128), 0)
    lanes = iota((32, 128), 1)

    def plane(p, before, is_last):
        q = [src[c, p] for c in range(4)]
        v = visc(p)
        if is_last:
            after = None
            total = [-b for b in before]
        else:
            after = flux(q, [src[c, p + 1] for c in range(4)], v, visc(p + 1), 0)
            total = after if before is None else [a - b for a, b in zip(after, before)]
        for axis, size, edge, d in ((0, 32, rows == 31, 1), (1, 128, lanes == 127, 2)):
            q_next = [pltpu.roll(x, size - 1, axis) for x in q]
            faces = flux(q, q_next, v, pltpu.roll(v, size - 1, axis), d)
            faces = [jnp.where(edge, 0.0, f) for f in faces]
            total = [t + (f - pltpu.roll(f, 1, axis)) for t, f in zip(total, faces)]
        out = [x - TIME_STEP * t for x, t in zip(q, total)]
        out[2] = out[2] + (TIME_STEP * BUOYANCY) * q[3]
        store(p, out)
        return after

    def body(p, before):
        return tuple(plane(p, before, False))

    before = lax.fori_loop(2, 8, body, tuple(plane(1, None, False)))
    plane(8, before, True)


def edge_z(dst, first, z_own, z_far, v_own, v_far):
    rows = iota((128, 128), 0)

    def face(ref, side):
        return [ref[side, 2 * c : 2 * c + 2] for c in range(4)]

    low = flux(face(z_far, 1), face(z_own, 0), v_far[1, 8:10], v_own[0, 8:10], 2)
    high = flux(face(z_own, 1), face(z_far, 0), v_own[1, 8:10], v_far[0, 8:10], 2)
    for c in range(4):
        for h in range(2):
            placed = jnp.where(
                rows == 0,
                TIME_STEP * low[c][h : h + 1],
                jnp.where(rows == 127, -TIME_STEP * high[c][h : h + 1], 0.0),
            )
            planes = slice(first + 4 * h, first + 4 * h + 4)
            dst[c, planes] = dst[c, planes] + placed.T.reshape(4, 32, 128)


def edge_x(src, visc, dst, first):
    def of(p):
        return [src[c, p] for c in range(4)]

    low = flux(of(0), of(1), visc(0), visc(1), 0)
    high = flux(of(8), of(9), visc(8), visc(9), 0)
    for c in range(4):
        dst[c, first] = dst[c, first] + TIME_STEP * low[c]
        dst[c, first + 7] = dst[c, first + 7] - TIME_STEP * high[c]


def edge_y(dst, first, y_own, y_far, v_own, v_far):
    def face(ref, side):
        return [ref[side, c] for c in range(4)]

    low = flux(face(y_far, 0), face(y_own, 0), v_far[0, 4], v_own[0, 4], 1)
    high = flux(face(y_own, 1), face(y_far, 1), v_own[1, 4], v_far[1, 4], 1)
    planes = slice(first, first + 8)
    for c in range(4):
        dst[c, planes, 0, :] = dst[c, planes, 0, :] + TIME_STEP * low[c]
        dst[c, planes, 31, :] = dst[c, planes, 31, :] - TIME_STEP * high[c]


def pack_y(src, count, y_send):
    for c in range(count):
        y_send[0, c] = src[c, 1:9, 0, :]
        y_send[1, c] = src[c, 1:9, 31, :]


def pack_z(src, count, z_send):
    for c in range(count):
        for h in range(2):
            turned = src[c, 1 + 4 * h : 5 + 4 * h].reshape(128, 128).T
            g = 2 * c + h
            z_send[0, g : g + 1, :] = turned[0:1]
            z_send[1, g : g + 1, :] = turned[127:128]


def by_lane(values, lanes_of):
    out = jnp.zeros(lanes_of.shape, I32)
    for j in range(8):
        out = jnp.where(lanes_of == j, values[j], out)
    return out


def shifts():
    return [(ox, oy) for ox in (-1, 0, 1) for oy in (-1, 0, 1)]


def inside(ox, oy):
    lanes = iota((1, 128), 1)
    x = lanes // 4 % 4 + ox
    y = lanes % 4 + oy
    return jnp.where((x >= 0) & (x < 4) & (y >= 0) & (y < 4), 1.0, 0.0)


def rolled(x, ox, oy):
    if ox == 0 and oy == 0:
        return x
    return pltpu.roll(x, (-(4 * ox + oy)) % 128, 1) * inside(ox, oy)


def box(x):
    rows = iota(x.shape, 0) % 4
    lanes = iota(x.shape, 1)
    count = x.shape[0]
    x = (
        x
        + jnp.where(rows > 0, pltpu.roll(x, 1, 0), 0.0)
        + jnp.where(rows < 3, pltpu.roll(x, count - 1, 0), 0.0)
    )
    for step, place in ((1, lanes % 4), (4, lanes // 4 % 4)):
        x = (
            x
            + jnp.where(place > 0, pltpu.roll(x, step, 1), 0.0)
            + jnp.where(place < 3, pltpu.roll(x, 128 - step, 1), 0.0)
        )
    return x / 27.0


def cat_rows(x):
    return jnp.concatenate([x[:, 128 * z : 128 * z + 128] for z in range(4)], axis=0)


def dot(a, b, dims=None, precision=None):
    if dims is None:
        dims = (((1,), (0,)), ((), ()))
    return lax.dot_general(a, b, dims, precision=precision, preferred_element_type=F32)


def whole_kernel(
    fields_hbm, visc_hbm, samples_hbm, trainers_hbm, w1_hbm, w2_hbm, w3_hbm,
    adv_hbm, loss_hbm, final,
    samples, trainers,
    start, mid, adv, y_send, y_recv, z_send, z_recv, y_send2, y_recv2, z_send2, z_recv2,
    t_send, t_recv, l_send, l_recv, w1, w2, w3, w2_turned, hot, keep, folds, st1, st2,
    grads, part, sum1, spread, sum2, loss_out,
    local_sem, x_s, x_r, y_s, y_r, z_s, z_r, x2_s, x2_r, y2_s, y2_r, z2_s, z2_r,
    t_s, t_r, l_s, l_r, a_s, a_r, b_s, b_r, c_s, c_r,
):
    ax = lax.axis_index("gx")
    ay = lax.axis_index("gy")
    az = lax.axis_index("gz")
    half = ay // 8
    az_seen = lax.rem(az + half, 2)
    aw = ax * NZ + az_seen

    def in_same(d):
        to = lax.rem(ay + d, NY)
        return (ax, to, lax.rem(az_seen + to // 8, 2))

    def in_y(d):
        return (ax, lax.rem(ay + d, NY), az)

    def in_w(d):
        w = lax.rem(aw + d, NX * NZ)
        return (w // NZ, ay, lax.rem(w + half, NZ))

    loads = [
        pltpu.make_async_copy(src, dst, local_sem.at[i])
        for i, (src, dst) in enumerate(
            (
                (fields_hbm, start.at[0:4, 1:9]),
                (visc_hbm, start.at[4, 1:9]),
                (trainers_hbm, trainers),
                (samples_hbm, samples),
                (w1_hbm, w1),
                (w2_hbm, w2),
                (w3_hbm, w3),
            )
        )
    ]
    loads[0].start()
    loads[1].start()
    barrier = pltpu.get_barrier_semaphore()

    def greet(d, carry):
        pl.semaphore_signal(barrier, inc=1, device_id=in_y(d), device_id_type=MESH)
        pl.semaphore_signal(barrier, inc=1, device_id=in_w(d), device_id_type=MESH)
        return carry

    lax.fori_loop(1, 16, greet, 0)

    def greet_mirrored(d, carry):
        to = lax.rem((1 - half) * 8 + d, NY)
        pl.semaphore_signal(barrier, inc=1, device_id=(ax, to, 1 - az), device_id_type=MESH)
        return carry

    lax.fori_loop(0, 8, greet_mirrored, 0)
    for load in loads[2:]:
        load.start()
    loads[0].wait()
    loads[1].wait()
    pack_y(start, 5, y_send)
    pack_z(start, 5, z_send)
    loads[2].wait()
    owners = [trainers[j] for j in range(8)]
    t_send[...] = by_lane(owners, iota((1, 128), 1) % 8)
    pl.semaphore_wait(barrier, 38)

    def remote(src, dst, s, r, to):
        return pltpu.make_async_remote_copy(
            src_ref=src, dst_ref=dst, send_sem=s, recv_sem=r, device_id=to, device_id_type=MESH
        )

    x_up = (lax.rem(ax + 1, NX), ay, az)
    x_down = (lax.rem(ax + NX - 1, NX), ay, az)
    other = (ax, ay, 1 - az)

    def exchange_x(ref, s, r):
        return [
            remote(ref.at[:, 8], ref.at[:, 0], s.at[0], r.at[0], x_up),
            remote(ref.at[:, 1], ref.at[:, 9], s.at[1], r.at[1], x_down),
        ]

    def exchange_y(ys, yr, s, r):
        return [
            remote(ys.at[1], yr.at[0], s.at[0], r.at[0], in_y(1)),
            remote(ys.at[0], yr.at[1], s.at[1], r.at[1], in_y(NY - 1)),
        ]

    def begin(moves):
        for move in moves:
            move.start()

    def finish(moves):
        for move in moves:
            move.wait()

    def everyone(src, buf, s, r, slot, to):
        def send(d, carry):
            remote(src, buf.at[slot], s.at[d], r.at[slot], to(d)).start()
            return carry

        lax.fori_loop(1, 16, send, 0)

    def all_here(src, buf, s, r, slot, to):
        def receive(d, carry):
            at = lax.rem(slot + d, 16)
            copy = remote(src, buf.at[at], s.at[d], r.at[at], to(d))
            copy.wait_send()
            copy.wait_recv()
            return carry

        lax.fori_loop(1, 16, receive, 0)

    moves_y = exchange_y(y_send, y_recv, y_s, y_r)
    moves_x = exchange_x(start, x_s, x_r)
    moves_z = [remote(z_send, z_recv, z_s, z_r, other)]
    begin(moves_y)
    begin(moves_x)
    begin(moves_z)
    everyone(t_send, t_recv, t_s, t_r, ay, in_y)
    t_recv[ay] = t_send[...]

    def visc(p):
        return start[4, p]

    def store_mid(p, out):
        for c in range(4):
            mid[c, p] = out[c]

    inner_part(start, visc, store_mid)
    loads[3].wait()
    picked = [samples[j] for j in range(8)]
    row = iota((128, 256), 0)
    base = by_lane([(s // 256) * 128 + (s // 32 % 8) * 4 for s in picked], row // 16)
    want = base + row // 4 % 4 * 32 + row % 4
    hot[...] = jnp.where(want == iota((128, 256), 1), 1.0, 0.0).astype(BF16)
    lanes128 = iota((128, 128), 1)
    lz = by_lane([s % 32 for s in picked], iota((128, 128), 0) // 16)
    keep[...] = jnp.where(lz == lanes128 // 4, 1.0, 0.0)
    finish(moves_z)
    edge_z(mid, 1, z_send, z_recv, z_send, z_recv)
    finish(moves_x)
    edge_x(start, visc, mid, 1)
    finish(moves_y)
    edge_y(mid, 1, y_send, y_recv, y_send, y_recv)

    pack_y(mid, 4, y_send2)
    moves_y = exchange_y(y_send2, y_recv2, y2_s, y2_r)
    begin(moves_y)
    moves_x = exchange_x(mid, x2_s, x2_r)
    begin(moves_x)
    pack_z(mid, 4, z_send2)
    moves_z = [remote(z_send2, z_recv2, z2_s, z2_r, other)]
    begin(moves_z)

    def store_adv(p, out):
        for c in range(4):
            adv[c, p - 1] = out[c]

    inner_part(mid, visc, store_adv)
    frow = iota((64, 128), 0)
    flane = iota((64, 128), 1)
    comp = frow % 4
    for i, c in enumerate(PAIR_P + PAIR_Q):
        here = (frow >= 16 + 4 * i) & (frow < 20 + 4 * i)
        comp = jnp.where(here, c, comp)
    zrow = jnp.where(frow < 16, frow // 4, frow % 4)
    for c in range(4):
        folds[c] = jnp.where((comp == c) & (flane % 4 == zrow), 1.0, 0.0).astype(BF16)
    for load in loads[4:]:
        load.wait()
    st1[...] = jnp.zeros_like(st1)
    st2[...] = jnp.zeros_like(st2)
    for t in range(7):
        width = 128 if t < 6 else 96
        turned = w2[:, 128 * t : 128 * t + width].astype(F32).T
        w2_turned[128 * t : 128 * t + width, :] = turned.astype(BF16)
    pick_row = jnp.where(iota((24, 6), 0) // 4 == iota((24, 6), 1), 1.0, 0.0).astype(BF16)
    pick_col = jnp.where(iota((32, 128), 1) % 32 == iota((32, 128), 0), 1.0, 0.0).astype(BF16)
    spread3 = dot(dot(pick_row, w3[...]).astype(BF16), pick_col)
    same_z = iota((24, 128), 0) % 4 == iota((24, 128), 1) // 32
    wide3 = jnp.where(same_z, spread3, 0.0).astype(BF16)
    all_here(t_send, t_recv, t_s, t_r, ay, in_y)
    owned = t_recv[:, 0, :]
    mine = by_lane(owners, iota((16, 128), 1) // 16)
    load = jnp.zeros((16, 128), F32)
    for s in range(8):
        other_owner = owned if s == 0 else pltpu.roll(owned, s, 1)
        load = load + jnp.where(other_owner == mine, 1.0, 0.0)
    load = jnp.sum(load, axis=0, keepdims=True)
    share = 1.0 / (WORKERS * jnp.maximum(load, 1.0))
    scale = share * (2.0 / 384.0)
    finish(moves_z)
    edge_z(adv, 0, z_send2, z_recv2, z_send, z_recv)
    finish(moves_x)
    edge_x(mid, visc, adv, 0)
    finish(moves_y)
    edge_y(adv, 0, y_send2, y_recv2, y_send, y_recv)
    write = pltpu.make_async_copy(adv, adv_hbm, local_sem.at[7])
    write.start()

    cells = jnp.zeros((64, 128), F32)
    for c in range(4):
        plane = adv[c].reshape(256, 128).astype(BF16)
        found = (dot(hot[...], plane) * keep[...]).astype(BF16)
        cells = cells + dot(folds[c], found, NT)

    chosen = cells[0:16]
    for i, (ox, oy) in enumerate(shifts()):
        moved = rolled(chosen, ox, oy)
        for o in range(3):
            k = 3 * i + o
            for z in range(4):
                if 0 <= z + o - 1 < 4:
                    st1[4 * k : 4 * k + 4, 128 * z : 128 * z + 128] = moved[
                        4 * (z + o - 1) : 4 * (z + o - 1) + 4
                    ]
    pre1 = cat_rows(dot(w1[...], st1[0:108, :].astype(BF16)))
    sig1 = jax.nn.sigmoid(pre1)
    slope1 = sig1 * (1.0 + pre1 * (1.0 - sig1))
    hid1 = (pre1 * sig1).astype(BF16).astype(F32)
    for i, (ox, oy) in enumerate(shifts()):
        moved = rolled(hid1, ox, oy).astype(BF16)
        for o in range(3):
            k = 3 * i + o
            for z in range(4):
                if 0 <= z + o - 1 < 4:
                    st2[32 * k : 32 * k + 32, 128 * z : 128 * z + 128] = moved[
                        32 * (z + o - 1) : 32 * (z + o)
                    ]
    pre2 = cat_rows(dot(w2[...], st2[0:864, :]))
    sig2 = jax.nn.sigmoid(pre2)
    slope2 = sig2 * (1.0 + pre2 * (1.0 - sig2))
    hid2 = (pre2 * sig2).astype(BF16)
    predicted = dot(wide3, hid2)
    up_p, up_q = cells[16:40], cells[40:64]
    smooth = box(jnp.concatenate([up_p * up_q, up_p, up_q], axis=0))
    misfit = predicted - (smooth[0:24] - smooth[24:48] * smooth[48:72])
    grad_pred = (misfit * scale).astype(BF16)

    third = jnp.where(same_z, dot(grad_pred, hid2, NT), 0.0)
    third = jnp.concatenate(
        [jnp.sum(third[4 * i : 4 * i + 4], axis=0, keepdims=True) for i in range(6)]
        + [jnp.zeros((26, 128), F32)],
        axis=0,
    )
    third = third + pltpu.roll(third, 32, 1)
    third = third + pltpu.roll(third, 64, 1)
    grad_mid = (dot(wide3, grad_pred, TN) * slope2).astype(BF16)
    mid_cols = jnp.concatenate([grad_mid[32 * z : 32 * z + 32] for z in range(4)], axis=1)

    def send_tile(i):
        for h in range(2):
            to = 2 * i + h

            @pl.when(aw != to)
            def _():
                remote(
                    grads.at[to], part.at[aw], a_s.at[to], a_r.at[aw], (to // NZ, ay, lax.rem(to + half, NZ))
                ).start()

    def store_tile(i, x):
        grads[2 * i] = x[0:16].astype(BF16)
        grads[2 * i + 1] = x[16:32].astype(BF16)

    for i in range(7):
        rows_here = 128 if i < 6 else 96
        tile = dot(mid_cols, st2[128 * i : 128 * i + rows_here, :], NT)
        if i == 6:
            tile = jnp.concatenate([tile, third[:, 96:128]], axis=1)
        store_tile(i, tile)
        send_tile(i)
    lower = jnp.zeros((128, 128), F32)
    for i, (ox, oy) in enumerate(shifts()):
        y = dot(w2_turned[96 * i : 96 * i + 96, :], mid_cols)
        parts = []
        for z in range(4):
            total = y[32:64, 128 * z : 128 * z + 128]
            if z + 1 < 4:
                total = total + y[0:32, 128 * z + 128 : 128 * z + 256]
            if z - 1 >= 0:
                total = total + y[64:96, 128 * z - 128 : 128 * z]
            parts.append(total)
        lower = lower + rolled(jnp.concatenate(parts, axis=0), -ox, -oy)
    entry = (lower * slope1).astype(BF16)
    entry_cols = jnp.concatenate([entry[32 * z : 32 * z + 32] for z in range(4)], axis=1)
    store_tile(7, dot(entry_cols, st1[...].astype(BF16), NT))
    send_tile(7)

    squares = jnp.broadcast_to(jnp.sum(misfit * misfit, axis=0, keepdims=True), (8, 128))
    group = jnp.where(iota((128, 128), 0) // 16 == lanes128 % 8, 1.0, 0.0)
    l_send[...] = dot(squares, group, precision=HIGH)[0:1] / 384.0
    everyone(l_send, l_recv, l_s, l_r, ay, in_y)
    l_recv[ay] = l_send[...]

    part[aw] = grads[aw]
    for to in range(16):

        @pl.when(aw != to)
        def _():
            remote(
                grads.at[to], part.at[to], a_s.at[to], a_r.at[to], (to // NZ, ay, lax.rem(to + half, NZ))
            ).wait()

    def added(buf):
        total = buf[0].astype(F32)
        for s in range(1, 16):
            total = total + buf[s].astype(F32)
        return total

    sum1[...] = added(part).astype(BF16)
    everyone(sum1, spread, b_s, b_r, ay, in_same)
    spread[ay] = sum1[...]

    all_here(l_send, l_recv, l_s, l_r, ay, in_y)
    lanes16 = iota((16, 128), 1)
    rank = jnp.zeros((16, 128), I32)
    for s in range(1, 8):
        earlier = (pltpu.roll(owned, s, 1) == owned) & (lanes16 % 8 >= s)
        rank = rank + jnp.where(earlier, 1, 0)
    losses = l_recv[:, 0, :]
    own = (owned == ay) & (lanes16 < 8)
    place = lanes16 - 2 * iota((16, 128), 0)
    slots = jnp.zeros((16, 128), F32)
    for r in range(2):
        value = jnp.sum(jnp.where(own & (rank == r), losses, 0.0), axis=1, keepdims=True)
        slots = slots + jnp.where(place == r, value, 0.0)
    loss_out[...] = jnp.sum(slots, axis=0, keepdims=True)[:, 0:32]
    write_loss = pltpu.make_async_copy(loss_out, loss_hbm, local_sem.at[8])
    write_loss.start()

    all_here(sum1, spread, b_s, b_r, ay, in_same)
    sum2[...] = added(spread).astype(BF16)
    everyone(sum2, final, c_s, c_r, aw, in_w)
    own_part = pltpu.make_async_copy(sum2, final.at[aw], local_sem.at[9])
    own_part.start()
    write.wait()
    write_loss.wait()
    own_part.wait()
    all_here(sum2, final, c_s, c_r, aw, in_w)


def hand_over_kernel(
    adv_in, loss_in, final_in, adv_out, loss_out, first_out, second_out, third_out,
    adv, loss, final, first, second, third, sem,
):
    load_final = pltpu.make_async_copy(final_in, final, sem.at[5])
    load_final.start()
    pieces = [(c, slice(4 * h, 4 * h + 4)) for c in range(4) for h in range(2)]
    loads = [
        pltpu.make_async_copy(adv_in.at[piece], adv.at[piece], sem.at[6 + i])
        for i, piece in enumerate(pieces)
    ]
    loads.append(pltpu.make_async_copy(loss_in, loss, sem.at[4]))
    for load in loads:
        load.start()
    load_final.wait()
    for i in range(6):
        second[:, 128 * i : 128 * i + 128] = final[2 * i : 2 * i + 2].astype(F32).reshape(32, 128)
    last = final[12:14].astype(F32).reshape(32, 128)
    second[:, 768:864] = last[:, 0:96]
    third[...] = last[0:6, 96:128]
    first[...] = final[14:16].astype(F32).reshape(32, 128)[:, 0:108]
    stores = [
        pltpu.make_async_copy(second, second_out, sem.at[0]),
        pltpu.make_async_copy(first, first_out, sem.at[1]),
        pltpu.make_async_copy(third, third_out, sem.at[2]),
    ]
    for store in stores:
        store.start()
    for i, piece in enumerate(pieces):
        loads[i].wait()
        stores.append(pltpu.make_async_copy(adv.at[piece], adv_out.at[piece], sem.at[14 + i]))
        stores[-1].start()
    loads[8].wait()
    stores.append(pltpu.make_async_copy(loss, loss_out, sem.at[3]))
    stores[-1].start()
    for store in stores:
        store.wait()


def on_device(fields, viscosity, samples, trainers, conv_first, conv_second, conv_third):
    hbm = pl.BlockSpec(memory_space=pl.ANY)
    dma = pltpu.SemaphoreType.DMA
    v = pltpu.VMEM
    shapes = (
        jax.ShapeDtypeStruct((4, 8, 32, 128), F32),
        jax.ShapeDtypeStruct((1, 32), F32),
        jax.ShapeDtypeStruct((32, 108), F32),
        jax.ShapeDtypeStruct((32, 864), F32),
        jax.ShapeDtypeStruct((6, 32), F32),
    )
    results = pl.pallas_call(
        whole_kernel,
        out_shape=(shapes[0], shapes[1], jax.ShapeDtypeStruct((16, 16, 128), BF16)),
        in_specs=[hbm] * 7,
        out_specs=(hbm,) * 3,
        scratch_shapes=[
            pltpu.SMEM((8,), I32), pltpu.SMEM((8,), I32),
            v((5, 10, 32, 128), F32), v((4, 10, 32, 128), F32), v((4, 8, 32, 128), F32),
            v((2, 5, 8, 128), F32), v((2, 5, 8, 128), F32),
            v((2, 16, 128), F32), v((2, 16, 128), F32),
            v((2, 4, 8, 128), F32), v((2, 4, 8, 128), F32),
            v((2, 8, 128), F32), v((2, 8, 128), F32),
            v((1, 128), I32), v((16, 1, 128), I32), v((1, 128), F32), v((16, 1, 128), F32),
            v((32, 108), BF16), v((32, 864), BF16), v((6, 32), BF16),
            v((864, 32), BF16), v((128, 256), BF16), v((128, 128), F32), v((4, 64, 128), BF16),
            v((128, 512), F32), v((864, 512), BF16),
            v((16, 16, 128), BF16), v((16, 16, 128), BF16), v((16, 128), BF16),
            v((16, 16, 128), BF16), v((16, 128), BF16), v((1, 32), F32),
            dma((10,)),
            dma((2,)), dma((2,)), dma((2,)), dma((2,)), dma, dma,
            dma((2,)), dma((2,)), dma((2,)), dma((2,)), dma, dma,
            dma((16,)), dma((16,)), dma((16,)), dma((16,)),
            dma((16,)), dma((16,)), dma((16,)), dma((16,)), dma((16,)), dma((16,)),
        ],
        compiler_params=pltpu.CompilerParams(
            collective_id=0, has_side_effects=True, vmem_limit_bytes=60 * 1024 * 1024
        ),
        name="step",
    )(
        fields, viscosity, samples.reshape(8), trainers.reshape(8),
        conv_first, conv_second, conv_third,
    )
    advanced, losses, first, second, third = pl.pallas_call(
        hand_over_kernel,
        out_shape=shapes,
        in_specs=[hbm] * 3,
        out_specs=(hbm,) * 5,
        scratch_shapes=[
            v((4, 8, 32, 128), F32), v((1, 32), F32), v((16, 16, 128), BF16),
            v((32, 108), F32), v((32, 864), F32), v((6, 32), F32), dma((22,)),
        ],
        compiler_params=pltpu.CompilerParams(vmem_limit_bytes=60 * 1024 * 1024),
        name="hand_over",
    )(*results)
    return advanced, losses.reshape(1, 1, 1, 32), first, second, third


def solution(mesh):
    in_specs = (
        P(None, "gx", "gy", "gz"),
        P("gx", "gy", "gz"),
        P("gx", "gy", "gz", None),
        P("gx", "gy", "gz", None, None),
        P(),
        P(),
        P(),
    )
    out_specs = (P(None, "gx", "gy", "gz"), P("gx", "gy", "gz", None), P(), P(), P())
    return jax.shard_map(
        on_device, mesh=mesh, in_specs=in_specs, out_specs=out_specs, check_vma=False
    )
```

```python
import jax
import jax.numpy as jnp
from jax import lax
from jax.experimental import pallas as pl
from jax.experimental.pallas import tpu as pltpu
from jax.sharding import PartitionSpec as P

MESH = pl.DeviceIdType.MESH
F32 = jnp.float32
BF16 = jnp.bfloat16
I32 = jnp.int32
HIGH = lax.Precision.HIGHEST

NX, NY, NZ = 8, 16, 2
WORKERS = NX * NY * NZ
NT = (((1,), (1,)), ((), ()))
TN = (((0,), (0,)), ((), ()))
TIME_STEP = 0.25
BUOYANCY = 0.5
FAR_Y = (4, 12, 3, 5, 11, 13, 2, 6, 10, 14, 1, 7, 9, 15, 8)
FAR_W = (8, 9, 10, 7, 11, 6, 5, 4, 12, 13, 14, 3, 2, 15, 1)
PAIR_P = (0, 1, 2, 0, 0, 1)
PAIR_Q = (0, 1, 2, 1, 2, 2)


def iota(shape, dim):
    return lax.broadcasted_iota(I32, shape, dim)


def flux(low, high, visc_low, visc_high, d):
    speed = 0.25 * (low[d] + high[d])
    visc = 0.5 * (visc_low + visc_high)
    return [speed * (a + b) - visc * (b - a) for a, b in zip(low, high)]


def inner_part(src, visc, store):
    rows = iota((32, 128), 0)
    lanes = iota((32, 128), 1)

    def plane(p, before, is_last):
        q = [src[c, p] for c in range(4)]
        v = visc(p)
        if is_last:
            after = None
            total = [-b for b in before]
        else:
            after = flux(q, [src[c, p + 1] for c in range(4)], v, visc(p + 1), 0)
            total = after if before is None else [a - b for a, b in zip(after, before)]
        for axis, size, edge, d in ((0, 32, rows == 31, 1), (1, 128, lanes == 127, 2)):
            q_next = [pltpu.roll(x, size - 1, axis) for x in q]
            faces = flux(q, q_next, v, pltpu.roll(v, size - 1, axis), d)
            faces = [jnp.where(edge, 0.0, f) for f in faces]
            total = [t + (f - pltpu.roll(f, 1, axis)) for t, f in zip(total, faces)]
        out = [x - TIME_STEP * t for x, t in zip(q, total)]
        out[2] = out[2] + (TIME_STEP * BUOYANCY) * q[3]
        store(p, out)
        return after

    def body(p, before):
        return tuple(plane(p, before, False))

    before = lax.fori_loop(2, 8, body, tuple(plane(1, None, False)))
    plane(8, before, True)


def edge_z(dst, first, z_own, z_far, v_own, v_far):
    rows = iota((128, 128), 0)

    def face(ref, side):
        return [ref[side, 2 * c : 2 * c + 2] for c in range(4)]

    low = flux(face(z_far, 1), face(z_own, 0), v_far[1, 8:10], v_own[0, 8:10], 2)
    high = flux(face(z_own, 1), face(z_far, 0), v_own[1, 8:10], v_far[0, 8:10], 2)
    for c in range(4):
        for h in range(2):
            placed = jnp.where(
                rows == 0,
                TIME_STEP * low[c][h : h + 1],
                jnp.where(rows == 127, -TIME_STEP * high[c][h : h + 1], 0.0),
            )
            planes = slice(first + 4 * h, first + 4 * h + 4)
            dst[c, planes] = dst[c, planes] + placed.T.reshape(4, 32, 128)


def edge_x(src, visc, dst, first):
    def of(p):
        return [src[c, p] for c in range(4)]

    low = flux(of(0), of(1), visc(0), visc(1), 0)
    high = flux(of(8), of(9), visc(8), visc(9), 0)
    for c in range(4):
        dst[c, first] = dst[c, first] + TIME_STEP * low[c]
        dst[c, first + 7] = dst[c, first + 7] - TIME_STEP * high[c]


def edge_y(dst, first, y_own, y_far, v_own, v_far):
    def face(ref, side):
        return [ref[side, c] for c in range(4)]

    low = flux(face(y_far, 0), face(y_own, 0), v_far[0, 4], v_own[0, 4], 1)
    high = flux(face(y_own, 1), face(y_far, 1), v_own[1, 4], v_far[1, 4], 1)
    planes = slice(first, first + 8)
    for c in range(4):
        dst[c, planes, 0, :] = dst[c, planes, 0, :] + TIME_STEP * low[c]
        dst[c, planes, 31, :] = dst[c, planes, 31, :] - TIME_STEP * high[c]


def pack_y(src, count, y_send):
    for c in range(count):
        y_send[0, c] = src[c, 1:9, 0, :]
        y_send[1, c] = src[c, 1:9, 31, :]


def pack_z(src, count, z_send):
    for c in range(count):
        for h in range(2):
            turned = src[c, 1 + 4 * h : 5 + 4 * h].reshape(128, 128).T
            g = 2 * c + h
            z_send[0, g : g + 1, :] = turned[0:1]
            z_send[1, g : g + 1, :] = turned[127:128]


def by_lane(values, lanes_of):
    out = jnp.zeros(lanes_of.shape, I32)
    for j in range(8):
        out = jnp.where(lanes_of == j, values[j], out)
    return out


def shifts():
    return [(ox, oy) for ox in (-1, 0, 1) for oy in (-1, 0, 1)]


def inside(ox, oy):
    lanes = iota((1, 128), 1)
    x = lanes // 4 % 4 + ox
    y = lanes % 4 + oy
    return jnp.where((x >= 0) & (x < 4) & (y >= 0) & (y < 4), 1.0, 0.0)


def rolled(x, ox, oy):
    if ox == 0 and oy == 0:
        return x
    return pltpu.roll(x, (-(4 * ox + oy)) % 128, 1) * inside(ox, oy)


def box(x):
    rows = iota(x.shape, 0) % 4
    lanes = iota(x.shape, 1)
    count = x.shape[0]
    x = (
        x
        + jnp.where(rows > 0, pltpu.roll(x, 1, 0), 0.0)
        + jnp.where(rows < 3, pltpu.roll(x, count - 1, 0), 0.0)
    )
    for step, place in ((1, lanes % 4), (4, lanes // 4 % 4)):
        x = (
            x
            + jnp.where(place > 0, pltpu.roll(x, step, 1), 0.0)
            + jnp.where(place < 3, pltpu.roll(x, 128 - step, 1), 0.0)
        )
    return x / 27.0


def cat_rows(x):
    return jnp.concatenate([x[:, 128 * z : 128 * z + 128] for z in range(4)], axis=0)


def dot(a, b, dims=None, precision=None):
    if dims is None:
        dims = (((1,), (0,)), ((), ()))
    return lax.dot_general(a, b, dims, precision=precision, preferred_element_type=F32)


def whole_kernel(
    fields_hbm, visc_hbm, samples_hbm, trainers_hbm, w1_hbm, w2_hbm, w3_hbm,
    adv_hbm, loss_hbm, final,
    samples, trainers,
    start, mid, adv, y_send, y_recv, z_send, z_recv, y_send2, y_recv2, z_send2, z_recv2,
    t_send, t_recv, l_send, l_recv, w1, w2, w3, w2_turned, hot, keep, folds, st1, st2,
    grads, part, sum1, spread, sum2, loss_out,
    local_sem, x_s, x_r, y_s, y_r, z_s, z_r, x2_s, x2_r, y2_s, y2_r, z2_s, z2_r,
    t_s, t_r, l_s, l_r, a_s, a_r, b_s, b_r, c_s, c_r,
):
    ax = lax.axis_index("gx")
    ay = lax.axis_index("gy")
    az = lax.axis_index("gz")
    half = ay // 8
    az_seen = lax.rem(az + half, 2)
    aw = ax * NZ + az_seen

    def in_same(d):
        to = lax.rem(ay + d, NY)
        return (ax, to, lax.rem(az_seen + to // 8, 2))

    def in_y(d):
        return (ax, lax.rem(ay + d, NY), az)

    def in_w(d):
        w = lax.rem(aw + d, NX * NZ)
        return (w // NZ, ay, lax.rem(w + half, NZ))

    loads = [
        pltpu.make_async_copy(src, dst, local_sem.at[i])
        for i, (src, dst) in enumerate(
            (
                (fields_hbm, start.at[0:4, 1:9]),
                (visc_hbm, start.at[4, 1:9]),
                (trainers_hbm, trainers),
                (samples_hbm, samples),
                (w1_hbm, w1),
                (w2_hbm, w2),
                (w3_hbm, w3),
            )
        )
    ]
    loads[0].start()
    loads[1].start()
    barrier = pltpu.get_barrier_semaphore()

    def greet(d, carry):
        pl.semaphore_signal(barrier, inc=1, device_id=in_y(d), device_id_type=MESH)
        pl.semaphore_signal(barrier, inc=1, device_id=in_w(d), device_id_type=MESH)
        return carry

    lax.fori_loop(1, 16, greet, 0)

    def greet_mirrored(d, carry):
        to = lax.rem((1 - half) * 8 + d, NY)
        pl.semaphore_signal(barrier, inc=1, device_id=(ax, to, 1 - az), device_id_type=MESH)
        return carry

    lax.fori_loop(0, 8, greet_mirrored, 0)
    for load in loads[2:]:
        load.start()
    loads[0].wait()
    loads[1].wait()
    pack_y(start, 5, y_send)
    pack_z(start, 5, z_send)
    loads[2].wait()
    owners = [trainers[j] for j in range(8)]
    t_send[...] = by_lane(owners, iota((1, 128), 1) % 8)
    pl.semaphore_wait(barrier, 38)

    def remote(src, dst, s, r, to):
        return pltpu.make_async_remote_copy(
            src_ref=src, dst_ref=dst, send_sem=s, recv_sem=r, device_id=to, device_id_type=MESH
        )

    x_up = (lax.rem(ax + 1, NX), ay, az)
    x_down = (lax.rem(ax + NX - 1, NX), ay, az)
    other = (ax, ay, 1 - az)

    def exchange_x(ref, s, r):
        return [
            remote(ref.at[:, 8], ref.at[:, 0], s.at[0], r.at[0], x_up),
            remote(ref.at[:, 1], ref.at[:, 9], s.at[1], r.at[1], x_down),
        ]

    def exchange_y(ys, yr, s, r):
        return [
            remote(ys.at[1], yr.at[0], s.at[0], r.at[0], in_y(1)),
            remote(ys.at[0], yr.at[1], s.at[1], r.at[1], in_y(NY - 1)),
        ]

    def begin(moves):
        for move in moves:
            move.start()

    def finish(moves):
        for move in moves:
            move.wait()

    def everyone(src, buf, s, r, slot, to, order):
        for d in order:
            remote(src, buf.at[slot], s, r, to(d)).start()

    def all_here(buf, s, r):
        others = buf.at[pl.ds(0, 15)]
        remote(others, others, s, r, other).wait_recv()

    def all_sent(buf, s, r):
        others = buf.at[pl.ds(0, 15)]
        remote(others, others, s, r, other).wait_send()

    moves_y = exchange_y(y_send, y_recv, y_s, y_r)
    moves_x = exchange_x(start, x_s, x_r)
    moves_z = [remote(z_send, z_recv, z_s, z_r, other)]
    begin(moves_y)
    begin(moves_x)
    begin(moves_z)
    everyone(t_send, t_recv, t_s, t_r, ay, in_y, FAR_Y)
    t_recv[ay] = t_send[...]

    def visc(p):
        return start[4, p]

    def store_mid(p, out):
        for c in range(4):
            mid[c, p] = out[c]

    inner_part(start, visc, store_mid)
    loads[3].wait()
    picked = [samples[j] for j in range(8)]
    row = iota((128, 256), 0)
    base = by_lane([(s // 256) * 128 + (s // 32 % 8) * 4 for s in picked], row // 16)
    want = base + row // 4 % 4 * 32 + row % 4
    hot[...] = jnp.where(want == iota((128, 256), 1), 1.0, 0.0).astype(BF16)
    lanes128 = iota((128, 128), 1)
    lz = by_lane([s % 32 for s in picked], iota((128, 128), 0) // 16)
    keep[...] = jnp.where(lz == lanes128 // 4, 1.0, 0.0)
    finish(moves_z)
    edge_z(mid, 1, z_send, z_recv, z_send, z_recv)
    finish(moves_x)
    edge_x(start, visc, mid, 1)
    finish(moves_y)
    edge_y(mid, 1, y_send, y_recv, y_send, y_recv)

    pack_y(mid, 4, y_send2)
    moves_y = exchange_y(y_send2, y_recv2, y2_s, y2_r)
    begin(moves_y)
    moves_x = exchange_x(mid, x2_s, x2_r)
    begin(moves_x)
    pack_z(mid, 4, z_send2)
    moves_z = [remote(z_send2, z_recv2, z2_s, z2_r, other)]
    begin(moves_z)

    def store_adv(p, out):
        for c in range(4):
            adv[c, p - 1] = out[c]

    inner_part(mid, visc, store_adv)
    frow = iota((64, 128), 0)
    flane = iota((64, 128), 1)
    comp = frow % 4
    for i, c in enumerate(PAIR_P + PAIR_Q):
        here = (frow >= 16 + 4 * i) & (frow < 20 + 4 * i)
        comp = jnp.where(here, c, comp)
    zrow = jnp.where(frow < 16, frow // 4, frow % 4)
    for c in range(4):
        folds[c] = jnp.where((comp == c) & (flane % 4 == zrow), 1.0, 0.0).astype(BF16)
    for load in loads[4:]:
        load.wait()
    st1[...] = jnp.zeros_like(st1)
    st2[...] = jnp.zeros_like(st2)
    for t in range(7):
        width = 128 if t < 6 else 96
        turned = w2[:, 128 * t : 128 * t + width].astype(F32).T
        w2_turned[128 * t : 128 * t + width, :] = turned.astype(BF16)
    pick_row = jnp.where(iota((24, 6), 0) // 4 == iota((24, 6), 1), 1.0, 0.0).astype(BF16)
    pick_col = jnp.where(iota((32, 128), 1) % 32 == iota((32, 128), 0), 1.0, 0.0).astype(BF16)
    spread3 = dot(dot(pick_row, w3[...]).astype(BF16), pick_col)
    same_z = iota((24, 128), 0) % 4 == iota((24, 128), 1) // 32
    wide3 = jnp.where(same_z, spread3, 0.0).astype(BF16)
    all_here(t_recv, t_s, t_r)
    owned = t_recv[:, 0, :]
    mine = by_lane(owners, iota((16, 128), 1) // 16)
    load = jnp.zeros((16, 128), F32)
    for s in range(8):
        other_owner = owned if s == 0 else pltpu.roll(owned, s, 1)
        load = load + jnp.where(other_owner == mine, 1.0, 0.0)
    load = jnp.sum(load, axis=0, keepdims=True)
    share = 1.0 / (WORKERS * jnp.maximum(load, 1.0))
    scale = share * (2.0 / 384.0)
    finish(moves_z)
    edge_z(adv, 0, z_send2, z_recv2, z_send, z_recv)
    finish(moves_x)
    edge_x(mid, visc, adv, 0)
    finish(moves_y)
    edge_y(adv, 0, y_send2, y_recv2, y_send, y_recv)
    write = pltpu.make_async_copy(adv, adv_hbm, local_sem.at[7])
    write.start()

    cells = jnp.zeros((64, 128), F32)
    for c in range(4):
        plane = adv[c].reshape(256, 128).astype(BF16)
        found = (dot(hot[...], plane) * keep[...]).astype(BF16)
        cells = cells + dot(folds[c], found, NT)

    chosen = cells[0:16]
    for i, (ox, oy) in enumerate(shifts()):
        moved = rolled(chosen, ox, oy)
        for o in range(3):
            k = 3 * i + o
            for z in range(4):
                if 0 <= z + o - 1 < 4:
                    st1[4 * k : 4 * k + 4, 128 * z : 128 * z + 128] = moved[
                        4 * (z + o - 1) : 4 * (z + o - 1) + 4
                    ]
    pre1 = cat_rows(dot(w1[...], st1[0:108, :].astype(BF16)))
    sig1 = jax.nn.sigmoid(pre1)
    slope1 = sig1 * (1.0 + pre1 * (1.0 - sig1))
    hid1 = (pre1 * sig1).astype(BF16).astype(F32)
    for i, (ox, oy) in enumerate(shifts()):
        moved = rolled(hid1, ox, oy).astype(BF16)
        for o in range(3):
            k = 3 * i + o
            for z in range(4):
                if 0 <= z + o - 1 < 4:
                    st2[32 * k : 32 * k + 32, 128 * z : 128 * z + 128] = moved[
                        32 * (z + o - 1) : 32 * (z + o)
                    ]
    pre2 = cat_rows(dot(w2[...], st2[0:864, :]))
    sig2 = jax.nn.sigmoid(pre2)
    slope2 = sig2 * (1.0 + pre2 * (1.0 - sig2))
    hid2 = (pre2 * sig2).astype(BF16)
    predicted = dot(wide3, hid2)
    up_p, up_q = cells[16:40], cells[40:64]
    smooth = box(jnp.concatenate([up_p * up_q, up_p, up_q], axis=0))
    misfit = predicted - (smooth[0:24] - smooth[24:48] * smooth[48:72])
    grad_pred = (misfit * scale).astype(BF16)

    third = jnp.where(same_z, dot(grad_pred, hid2, NT), 0.0)
    third = jnp.concatenate(
        [jnp.sum(third[4 * i : 4 * i + 4], axis=0, keepdims=True) for i in range(6)]
        + [jnp.zeros((26, 128), F32)],
        axis=0,
    )
    third = third + pltpu.roll(third, 32, 1)
    third = third + pltpu.roll(third, 64, 1)
    grad_mid = (dot(wide3, grad_pred, TN) * slope2).astype(BF16)
    mid_cols = jnp.concatenate([grad_mid[32 * z : 32 * z + 32] for z in range(4)], axis=1)

    def send_tile(i):
        for h in range(2):
            to = 2 * i + h

            @pl.when(aw != to)
            def _():
                remote(
                    grads.at[to], part.at[aw], a_s, a_r, (to // NZ, ay, lax.rem(to + half, NZ))
                ).start()

    def store_tile(i, x):
        grads[2 * i] = x[0:16].astype(BF16)
        grads[2 * i + 1] = x[16:32].astype(BF16)

    for i in range(7):
        rows_here = 128 if i < 6 else 96
        tile = dot(mid_cols, st2[128 * i : 128 * i + rows_here, :], NT)
        if i == 6:
            tile = jnp.concatenate([tile, third[:, 96:128]], axis=1)
        store_tile(i, tile)
        send_tile(i)
    lower = jnp.zeros((128, 128), F32)
    for i, (ox, oy) in enumerate(shifts()):
        y = dot(w2_turned[96 * i : 96 * i + 96, :], mid_cols)
        parts = []
        for z in range(4):
            total = y[32:64, 128 * z : 128 * z + 128]
            if z + 1 < 4:
                total = total + y[0:32, 128 * z + 128 : 128 * z + 256]
            if z - 1 >= 0:
                total = total + y[64:96, 128 * z - 128 : 128 * z]
            parts.append(total)
        lower = lower + rolled(jnp.concatenate(parts, axis=0), -ox, -oy)
    entry = (lower * slope1).astype(BF16)
    entry_cols = jnp.concatenate([entry[32 * z : 32 * z + 32] for z in range(4)], axis=1)
    store_tile(7, dot(entry_cols, st1[...].astype(BF16), NT))
    send_tile(7)

    squares = jnp.broadcast_to(jnp.sum(misfit * misfit, axis=0, keepdims=True), (8, 128))
    group = jnp.where(iota((128, 128), 0) // 16 == lanes128 % 8, 1.0, 0.0)
    l_send[...] = dot(squares, group, precision=HIGH)[0:1] / 384.0
    everyone(l_send, l_recv, l_s, l_r, ay, in_y, FAR_Y)
    l_recv[ay] = l_send[...]

    part[aw] = grads[aw]
    all_here(part, a_s, a_r)

    def added(buf):
        total = buf[0].astype(F32)
        for s in range(1, 16):
            total = total + buf[s].astype(F32)
        return total

    sum1[...] = added(part).astype(BF16)
    everyone(sum1, spread, b_s, b_r, ay, in_same, FAR_Y)
    spread[ay] = sum1[...]

    all_here(l_recv, l_s, l_r)
    lanes16 = iota((16, 128), 1)
    rank = jnp.zeros((16, 128), I32)
    for s in range(1, 8):
        earlier = (pltpu.roll(owned, s, 1) == owned) & (lanes16 % 8 >= s)
        rank = rank + jnp.where(earlier, 1, 0)
    losses = l_recv[:, 0, :]
    own = (owned == ay) & (lanes16 < 8)
    place = lanes16 - 2 * iota((16, 128), 0)
    slots = jnp.zeros((16, 128), F32)
    for r in range(2):
        value = jnp.sum(jnp.where(own & (rank == r), losses, 0.0), axis=1, keepdims=True)
        slots = slots + jnp.where(place == r, value, 0.0)
    loss_out[...] = jnp.sum(slots, axis=0, keepdims=True)[:, 0:32]
    write_loss = pltpu.make_async_copy(loss_out, loss_hbm, local_sem.at[8])
    write_loss.start()

    all_here(spread, b_s, b_r)
    sum2[...] = added(spread).astype(BF16)
    everyone(sum2, final, c_s, c_r, aw, in_w, FAR_W)
    own_part = pltpu.make_async_copy(sum2, final.at[aw], local_sem.at[9])
    own_part.start()
    write.wait()
    write_loss.wait()
    own_part.wait()
    for buf, s, r in (
        (t_recv, t_s, t_r), (l_recv, l_s, l_r), (part, a_s, a_r), (spread, b_s, b_r),
        (final, c_s, c_r),
    ):
        all_sent(buf, s, r)
    all_here(final, c_s, c_r)


def hand_over_kernel(
    adv_in, loss_in, final_in, adv_out, loss_out, first_out, second_out, third_out,
    adv, loss, final, first, second, third, sem,
):
    load_final = pltpu.make_async_copy(final_in, final, sem.at[5])
    load_final.start()
    pieces = [(c, slice(4 * h, 4 * h + 4)) for c in range(4) for h in range(2)]
    loads = [
        pltpu.make_async_copy(adv_in.at[piece], adv.at[piece], sem.at[6 + i])
        for i, piece in enumerate(pieces)
    ]
    loads.append(pltpu.make_async_copy(loss_in, loss, sem.at[4]))
    for load in loads:
        load.start()
    load_final.wait()
    for i in range(6):
        second[:, 128 * i : 128 * i + 128] = final[2 * i : 2 * i + 2].astype(F32).reshape(32, 128)
    last = final[12:14].astype(F32).reshape(32, 128)
    second[:, 768:864] = last[:, 0:96]
    third[...] = last[0:6, 96:128]
    first[...] = final[14:16].astype(F32).reshape(32, 128)[:, 0:108]
    stores = [
        pltpu.make_async_copy(second, second_out, sem.at[0]),
        pltpu.make_async_copy(first, first_out, sem.at[1]),
        pltpu.make_async_copy(third, third_out, sem.at[2]),
    ]
    for store in stores:
        store.start()
    for i, piece in enumerate(pieces):
        loads[i].wait()
        stores.append(pltpu.make_async_copy(adv.at[piece], adv_out.at[piece], sem.at[14 + i]))
        stores[-1].start()
    loads[8].wait()
    stores.append(pltpu.make_async_copy(loss, loss_out, sem.at[3]))
    stores[-1].start()
    for store in stores:
        store.wait()


def on_device(fields, viscosity, samples, trainers, conv_first, conv_second, conv_third):
    hbm = pl.BlockSpec(memory_space=pl.ANY)
    dma = pltpu.SemaphoreType.DMA
    v = pltpu.VMEM
    shapes = (
        jax.ShapeDtypeStruct((4, 8, 32, 128), F32),
        jax.ShapeDtypeStruct((1, 32), F32),
        jax.ShapeDtypeStruct((32, 108), F32),
        jax.ShapeDtypeStruct((32, 864), F32),
        jax.ShapeDtypeStruct((6, 32), F32),
    )
    results = pl.pallas_call(
        whole_kernel,
        out_shape=(shapes[0], shapes[1], jax.ShapeDtypeStruct((16, 16, 128), BF16)),
        in_specs=[hbm] * 7,
        out_specs=(hbm,) * 3,
        scratch_shapes=[
            pltpu.SMEM((8,), I32), pltpu.SMEM((8,), I32),
            v((5, 10, 32, 128), F32), v((4, 10, 32, 128), F32), v((4, 8, 32, 128), F32),
            v((2, 5, 8, 128), F32), v((2, 5, 8, 128), F32),
            v((2, 16, 128), F32), v((2, 16, 128), F32),
            v((2, 4, 8, 128), F32), v((2, 4, 8, 128), F32),
            v((2, 8, 128), F32), v((2, 8, 128), F32),
            v((1, 128), I32), v((16, 1, 128), I32), v((1, 128), F32), v((16, 1, 128), F32),
            v((32, 108), BF16), v((32, 864), BF16), v((6, 32), BF16),
            v((864, 32), BF16), v((128, 256), BF16), v((128, 128), F32), v((4, 64, 128), BF16),
            v((128, 512), F32), v((864, 512), BF16),
            v((16, 16, 128), BF16), v((16, 16, 128), BF16), v((16, 128), BF16),
            v((16, 16, 128), BF16), v((16, 128), BF16), v((1, 32), F32),
            dma((10,)),
            dma((2,)), dma((2,)), dma((2,)), dma((2,)), dma, dma,
            dma((2,)), dma((2,)), dma((2,)), dma((2,)), dma, dma,
            dma, dma, dma, dma, dma, dma, dma, dma, dma, dma,
        ],
        compiler_params=pltpu.CompilerParams(
            collective_id=0, has_side_effects=True, vmem_limit_bytes=60 * 1024 * 1024
        ),
        name="step",
    )(
        fields, viscosity, samples.reshape(8), trainers.reshape(8),
        conv_first, conv_second, conv_third,
    )
    advanced, losses, first, second, third = pl.pallas_call(
        hand_over_kernel,
        out_shape=shapes,
        in_specs=[hbm] * 3,
        out_specs=(hbm,) * 5,
        scratch_shapes=[
            v((4, 8, 32, 128), F32), v((1, 32), F32), v((16, 16, 128), BF16),
            v((32, 108), F32), v((32, 864), F32), v((6, 32), F32), dma((22,)),
        ],
        compiler_params=pltpu.CompilerParams(vmem_limit_bytes=60 * 1024 * 1024),
        name="hand_over",
    )(*results)
    return advanced, losses.reshape(1, 1, 1, 32), first, second, third


def solution(mesh):
    in_specs = (
        P(None, "gx", "gy", "gz"),
        P("gx", "gy", "gz"),
        P("gx", "gy", "gz", None),
        P("gx", "gy", "gz", None, None),
        P(),
        P(),
        P(),
    )
    out_specs = (P(None, "gx", "gy", "gz"), P("gx", "gy", "gz", None), P(), P(), P())
    return jax.shard_map(
        on_device, mesh=mesh, in_specs=in_specs, out_specs=out_specs, check_vma=False
    )
```

```python
import jax
import jax.numpy as jnp
from jax import lax
from jax.experimental import pallas as pl
from jax.experimental.pallas import tpu as pltpu
from jax.sharding import PartitionSpec as P

MESH = pl.DeviceIdType.MESH
F32 = jnp.float32
BF16 = jnp.bfloat16
I32 = jnp.int32
HIGH = lax.Precision.HIGHEST

NX, NY, NZ = 8, 16, 2
WORKERS = NX * NY * NZ
NT = (((1,), (1,)), ((), ()))
TN = (((0,), (0,)), ((), ()))
TIME_STEP = 0.25
BUOYANCY = 0.5
FAR_Y = (4, 12, 3, 5, 11, 13, 2, 6, 10, 14, 1, 7, 9, 15, 8)
FAR_W = (8, 9, 10, 7, 11, 6, 5, 4, 12, 13, 14, 3, 2, 15, 1)
PAIR_P = (0, 1, 2, 0, 0, 1)
PAIR_Q = (0, 1, 2, 1, 2, 2)


def iota(shape, dim):
    return lax.broadcasted_iota(I32, shape, dim)


def flux(low, high, visc_low, visc_high, d):
    speed = 0.25 * (low[d] + high[d])
    visc = 0.5 * (visc_low + visc_high)
    return [speed * (a + b) - visc * (b - a) for a, b in zip(low, high)]


def inner_part(src, visc, store):
    rows = iota((32, 128), 0)
    lanes = iota((32, 128), 1)

    def plane(p, before, is_last):
        q = [src[c, p] for c in range(4)]
        v = visc(p)
        if is_last:
            after = None
            total = [-b for b in before]
        else:
            after = flux(q, [src[c, p + 1] for c in range(4)], v, visc(p + 1), 0)
            total = after if before is None else [a - b for a, b in zip(after, before)]
        for axis, size, edge, d in ((0, 32, rows == 31, 1), (1, 128, lanes == 127, 2)):
            q_next = [pltpu.roll(x, size - 1, axis) for x in q]
            faces = flux(q, q_next, v, pltpu.roll(v, size - 1, axis), d)
            faces = [jnp.where(edge, 0.0, f) for f in faces]
            total = [t + (f - pltpu.roll(f, 1, axis)) for t, f in zip(total, faces)]
        out = [x - TIME_STEP * t for x, t in zip(q, total)]
        out[2] = out[2] + (TIME_STEP * BUOYANCY) * q[3]
        store(p, out)
        return after

    def body(p, before):
        return tuple(plane(p, before, False))

    before = lax.fori_loop(2, 8, body, tuple(plane(1, None, False)))
    plane(8, before, True)


def edge_z(dst, first, z_own, z_far, v_own, v_far):
    rows = iota((128, 128), 0)

    def face(ref, side):
        return [ref[side, 2 * c : 2 * c + 2] for c in range(4)]

    low = flux(face(z_far, 1), face(z_own, 0), v_far[1, 8:10], v_own[0, 8:10], 2)
    high = flux(face(z_own, 1), face(z_far, 0), v_own[1, 8:10], v_far[0, 8:10], 2)
    for c in range(4):
        for h in range(2):
            placed = jnp.where(
                rows == 0,
                TIME_STEP * low[c][h : h + 1],
                jnp.where(rows == 127, -TIME_STEP * high[c][h : h + 1], 0.0),
            )
            planes = slice(first + 4 * h, first + 4 * h + 4)
            dst[c, planes] = dst[c, planes] + placed.T.reshape(4, 32, 128)


def edge_x(src, visc, dst, first):
    def of(p):
        return [src[c, p] for c in range(4)]

    low = flux(of(0), of(1), visc(0), visc(1), 0)
    high = flux(of(8), of(9), visc(8), visc(9), 0)
    for c in range(4):
        dst[c, first] = dst[c, first] + TIME_STEP * low[c]
        dst[c, first + 7] = dst[c, first + 7] - TIME_STEP * high[c]


def edge_y(dst, first, y_own, y_far, v_own, v_far):
    def face(ref, side):
        return [ref[side, c] for c in range(4)]

    low = flux(face(y_far, 0), face(y_own, 0), v_far[0, 4], v_own[0, 4], 1)
    high = flux(face(y_own, 1), face(y_far, 1), v_own[1, 4], v_far[1, 4], 1)
    planes = slice(first, first + 8)
    for c in range(4):
        dst[c, planes, 0, :] = dst[c, planes, 0, :] + TIME_STEP * low[c]
        dst[c, planes, 31, :] = dst[c, planes, 31, :] - TIME_STEP * high[c]


def pack_y(src, count, y_send):
    for c in range(count):
        y_send[0, c] = src[c, 1:9, 0, :]
        y_send[1, c] = src[c, 1:9, 31, :]


def pack_z(src, count, z_send):
    for c in range(count):
        for h in range(2):
            turned = src[c, 1 + 4 * h : 5 + 4 * h].reshape(128, 128).T
            g = 2 * c + h
            z_send[0, g : g + 1, :] = turned[0:1]
            z_send[1, g : g + 1, :] = turned[127:128]


def by_lane(values, lanes_of):
    out = jnp.zeros(lanes_of.shape, I32)
    for j in range(8):
        out = jnp.where(lanes_of == j, values[j], out)
    return out


def shifts():
    return [(ox, oy) for ox in (-1, 0, 1) for oy in (-1, 0, 1)]


def inside(ox, oy):
    lanes = iota((1, 128), 1)
    x = lanes // 4 % 4 + ox
    y = lanes % 4 + oy
    return jnp.where((x >= 0) & (x < 4) & (y >= 0) & (y < 4), 1.0, 0.0)


def rolled(x, ox, oy):
    if ox == 0 and oy == 0:
        return x
    return pltpu.roll(x, (-(4 * ox + oy)) % 128, 1) * inside(ox, oy)


def box(x):
    rows = iota(x.shape, 0) % 4
    lanes = iota(x.shape, 1)
    count = x.shape[0]
    x = (
        x
        + jnp.where(rows > 0, pltpu.roll(x, 1, 0), 0.0)
        + jnp.where(rows < 3, pltpu.roll(x, count - 1, 0), 0.0)
    )
    for step, place in ((1, lanes % 4), (4, lanes // 4 % 4)):
        x = (
            x
            + jnp.where(place > 0, pltpu.roll(x, step, 1), 0.0)
            + jnp.where(place < 3, pltpu.roll(x, 128 - step, 1), 0.0)
        )
    return x / 27.0


def cat_rows(x):
    return jnp.concatenate([x[:, 128 * z : 128 * z + 128] for z in range(4)], axis=0)


def dot(a, b, dims=None, precision=None):
    if dims is None:
        dims = (((1,), (0,)), ((), ()))
    return lax.dot_general(a, b, dims, precision=precision, preferred_element_type=F32)


def whole_kernel(
    fields_hbm, visc_hbm, samples_hbm, trainers_hbm, w1_hbm, w2_hbm, w3_hbm,
    adv_hbm, loss_hbm, final,
    samples, trainers,
    start, mid, adv, y_send, y_recv, z_send, z_recv, y_send2, y_recv2, z_send2, z_recv2,
    t_send, t_recv, l_send, l_recv, w1, w2, w3, w2_turned, hot, keep, folds, st1, st2,
    grads, part, sum1, spread, sum2, loss_out,
    local_sem, x_s, x_r, y_s, y_r, z_s, z_r, x2_s, x2_r, y2_s, y2_r, z2_s, z2_r,
    t_s, t_r, l_s, l_r, a_s, a_r, b_s, b_r, c_s, c_r,
):
    ax = lax.axis_index("gx")
    ay = lax.axis_index("gy")
    az = lax.axis_index("gz")
    half = ay // 8
    az_seen = lax.rem(az + half, 2)
    aw = ax * NZ + az_seen

    def in_same(d):
        to = lax.rem(ay + d, NY)
        return (ax, to, lax.rem(az_seen + to // 8, 2))

    def in_y(d):
        return (ax, lax.rem(ay + d, NY), az)

    def in_w(d):
        w = lax.rem(aw + d, NX * NZ)
        return (w // NZ, ay, lax.rem(w + half, NZ))

    loads = [
        pltpu.make_async_copy(src, dst, local_sem.at[i])
        for i, (src, dst) in enumerate(
            (
                (fields_hbm, start.at[0:4, 1:9]),
                (visc_hbm, start.at[4, 1:9]),
                (trainers_hbm, trainers),
                (samples_hbm, samples),
                (w1_hbm, w1),
                (w2_hbm, w2),
                (w3_hbm, w3),
            )
        )
    ]
    loads[0].start()
    loads[1].start()
    barrier = pltpu.get_barrier_semaphore()

    def greet(d, carry):
        pl.semaphore_signal(barrier, inc=1, device_id=in_y(d), device_id_type=MESH)
        pl.semaphore_signal(barrier, inc=1, device_id=in_w(d), device_id_type=MESH)
        return carry

    lax.fori_loop(1, 16, greet, 0)

    def greet_mirrored(d, carry):
        to = lax.rem((1 - half) * 8 + d, NY)
        pl.semaphore_signal(barrier, inc=1, device_id=(ax, to, 1 - az), device_id_type=MESH)
        return carry

    lax.fori_loop(0, 8, greet_mirrored, 0)
    for load in loads[2:]:
        load.start()
    loads[0].wait()
    loads[1].wait()
    pack_y(start, 5, y_send)
    pack_z(start, 5, z_send)
    loads[2].wait()
    owners = [trainers[j] for j in range(8)]
    t_send[...] = by_lane(owners, iota((1, 128), 1) % 8)
    pl.semaphore_wait(barrier, 38)

    def remote(src, dst, s, r, to):
        return pltpu.make_async_remote_copy(
            src_ref=src, dst_ref=dst, send_sem=s, recv_sem=r, device_id=to, device_id_type=MESH
        )

    x_up = (lax.rem(ax + 1, NX), ay, az)
    x_down = (lax.rem(ax + NX - 1, NX), ay, az)
    other = (ax, ay, 1 - az)

    def exchange_x(ref, s, r):
        return [
            remote(ref.at[:, 8], ref.at[:, 0], s.at[0], r.at[0], x_up),
            remote(ref.at[:, 1], ref.at[:, 9], s.at[1], r.at[1], x_down),
        ]

    def exchange_y(ys, yr, s, r):
        return [
            remote(ys.at[1], yr.at[0], s.at[0], r.at[0], in_y(1)),
            remote(ys.at[0], yr.at[1], s.at[1], r.at[1], in_y(NY - 1)),
        ]

    def begin(moves):
        for move in moves:
            move.start()

    def finish(moves):
        for move in moves:
            move.wait()

    def everyone(src, buf, s, r, slot, to, order):
        for d in order:
            remote(src, buf.at[slot], s, r, to(d)).start()

    def all_here(buf, s, r):
        others = buf.at[pl.ds(0, 15)]
        remote(others, others, s, r, other).wait_recv()

    def all_sent(buf, s, r):
        others = buf.at[pl.ds(0, 15)]
        remote(others, others, s, r, other).wait_send()

    moves_y = exchange_y(y_send, y_recv, y_s, y_r)
    moves_x = exchange_x(start, x_s, x_r)
    moves_z = [remote(z_send, z_recv, z_s, z_r, other)]
    begin(moves_y)
    begin(moves_x)
    begin(moves_z)
    everyone(t_send, t_recv, t_s, t_r, ay, in_y, FAR_Y)
    t_recv[ay] = t_send[...]

    def visc(p):
        return start[4, p]

    def store_mid(p, out):
        for c in range(4):
            mid[c, p] = out[c]

    inner_part(start, visc, store_mid)
    loads[3].wait()
    picked = [samples[j] for j in range(8)]
    row = iota((128, 256), 0)
    base = by_lane([(s // 256) * 128 + (s // 32 % 8) * 4 for s in picked], row // 16)
    want = base + row // 4 % 4 * 32 + row % 4
    hot[...] = jnp.where(want == iota((128, 256), 1), 1.0, 0.0).astype(BF16)
    lanes128 = iota((128, 128), 1)
    lz = by_lane([s % 32 for s in picked], iota((128, 128), 0) // 16)
    keep[...] = jnp.where(lz == lanes128 // 4, 1.0, 0.0)
    finish(moves_z)
    edge_z(mid, 1, z_send, z_recv, z_send, z_recv)
    finish(moves_x)
    edge_x(start, visc, mid, 1)
    finish(moves_y)
    edge_y(mid, 1, y_send, y_recv, y_send, y_recv)

    pack_y(mid, 4, y_send2)
    moves_y = exchange_y(y_send2, y_recv2, y2_s, y2_r)
    begin(moves_y)
    moves_x = exchange_x(mid, x2_s, x2_r)
    begin(moves_x)
    pack_z(mid, 4, z_send2)
    moves_z = [remote(z_send2, z_recv2, z2_s, z2_r, other)]
    begin(moves_z)

    def store_adv(p, out):
        for c in range(4):
            adv[c, p - 1] = out[c]

    inner_part(mid, visc, store_adv)
    frow = iota((64, 128), 0)
    flane = iota((64, 128), 1)
    comp = frow % 4
    for i, c in enumerate(PAIR_P + PAIR_Q):
        here = (frow >= 16 + 4 * i) & (frow < 20 + 4 * i)
        comp = jnp.where(here, c, comp)
    zrow = jnp.where(frow < 16, frow // 4, frow % 4)
    for c in range(4):
        folds[c] = jnp.where((comp == c) & (flane % 4 == zrow), 1.0, 0.0).astype(BF16)
    for load in loads[4:]:
        load.wait()
    st1[...] = jnp.zeros_like(st1)
    st2[...] = jnp.zeros_like(st2)
    for t in range(7):
        width = 128 if t < 6 else 96
        turned = w2[:, 128 * t : 128 * t + width].astype(F32).T
        w2_turned[128 * t : 128 * t + width, :] = turned.astype(BF16)
    pick_row = jnp.where(iota((24, 6), 0) // 4 == iota((24, 6), 1), 1.0, 0.0).astype(BF16)
    pick_col = jnp.where(iota((32, 128), 1) % 32 == iota((32, 128), 0), 1.0, 0.0).astype(BF16)
    spread3 = dot(dot(pick_row, w3[...]).astype(BF16), pick_col)
    same_z = iota((24, 128), 0) % 4 == iota((24, 128), 1) // 32
    wide3 = jnp.where(same_z, spread3, 0.0).astype(BF16)
    all_here(t_recv, t_s, t_r)
    owned = t_recv[:, 0, :]
    mine = by_lane(owners, iota((16, 128), 1) // 16)
    load = jnp.zeros((16, 128), F32)
    for s in range(8):
        other_owner = owned if s == 0 else pltpu.roll(owned, s, 1)
        load = load + jnp.where(other_owner == mine, 1.0, 0.0)
    load = jnp.sum(load, axis=0, keepdims=True)
    share = 1.0 / (WORKERS * jnp.maximum(load, 1.0))
    scale = share * (2.0 / 384.0)
    finish(moves_z)
    edge_z(adv, 0, z_send2, z_recv2, z_send, z_recv)
    finish(moves_x)
    edge_x(mid, visc, adv, 0)
    finish(moves_y)
    edge_y(adv, 0, y_send2, y_recv2, y_send, y_recv)
    write = pltpu.make_async_copy(adv, adv_hbm, local_sem.at[7])
    write.start()

    cells = jnp.zeros((64, 128), F32)
    for c in range(4):
        plane = adv[c].reshape(256, 128).astype(BF16)
        found = (dot(hot[...], plane) * keep[...]).astype(BF16)
        cells = cells + dot(folds[c], found, NT)

    chosen = cells[0:16]
    for i, (ox, oy) in enumerate(shifts()):
        moved = rolled(chosen, ox, oy)
        for o in range(3):
            k = 3 * i + o
            for z in range(4):
                if 0 <= z + o - 1 < 4:
                    st1[4 * k : 4 * k + 4, 128 * z : 128 * z + 128] = moved[
                        4 * (z + o - 1) : 4 * (z + o - 1) + 4
                    ]
    pre1 = cat_rows(dot(w1[...], st1[0:108, :].astype(BF16)))
    sig1 = jax.nn.sigmoid(pre1)
    slope1 = sig1 * (1.0 + pre1 * (1.0 - sig1))
    hid1 = (pre1 * sig1).astype(BF16).astype(F32)
    for i, (ox, oy) in enumerate(shifts()):
        moved = rolled(hid1, ox, oy).astype(BF16)
        for o in range(3):
            k = 3 * i + o
            for z in range(4):
                if 0 <= z + o - 1 < 4:
                    st2[32 * k : 32 * k + 32, 128 * z : 128 * z + 128] = moved[
                        32 * (z + o - 1) : 32 * (z + o)
                    ]
    pre2 = cat_rows(dot(w2[...], st2[0:864, :]))
    sig2 = jax.nn.sigmoid(pre2)
    slope2 = sig2 * (1.0 + pre2 * (1.0 - sig2))
    hid2 = (pre2 * sig2).astype(BF16)
    predicted = dot(wide3, hid2)
    up_p, up_q = cells[16:40], cells[40:64]
    smooth = box(jnp.concatenate([up_p * up_q, up_p, up_q], axis=0))
    misfit = predicted - (smooth[0:24] - smooth[24:48] * smooth[48:72])
    grad_pred = (misfit * scale).astype(BF16)

    third = jnp.where(same_z, dot(grad_pred, hid2, NT), 0.0)
    third = jnp.concatenate(
        [jnp.sum(third[4 * i : 4 * i + 4], axis=0, keepdims=True) for i in range(6)]
        + [jnp.zeros((26, 128), F32)],
        axis=0,
    )
    third = third + pltpu.roll(third, 32, 1)
    third = third + pltpu.roll(third, 64, 1)
    grad_mid = (dot(wide3, grad_pred, TN) * slope2).astype(BF16)
    mid_cols = jnp.concatenate([grad_mid[32 * z : 32 * z + 32] for z in range(4)], axis=1)

    def store_tile(i, x):
        grads[2 * i] = x[0:16].astype(BF16)
        grads[2 * i + 1] = x[16:32].astype(BF16)

    lower = jnp.zeros((128, 128), F32)
    for i, (ox, oy) in enumerate(shifts()):
        y = dot(w2_turned[96 * i : 96 * i + 96, :], mid_cols)
        parts = []
        for z in range(4):
            total = y[32:64, 128 * z : 128 * z + 128]
            if z + 1 < 4:
                total = total + y[0:32, 128 * z + 128 : 128 * z + 256]
            if z - 1 >= 0:
                total = total + y[64:96, 128 * z - 128 : 128 * z]
            parts.append(total)
        lower = lower + rolled(jnp.concatenate(parts, axis=0), -ox, -oy)
    entry = (lower * slope1).astype(BF16)
    entry_cols = jnp.concatenate([entry[32 * z : 32 * z + 32] for z in range(4)], axis=1)
    store_tile(7, dot(entry_cols, st1[...].astype(BF16), NT))
    for i in range(7):
        rows_here = 128 if i < 6 else 96
        tile = dot(mid_cols, st2[128 * i : 128 * i + rows_here, :], NT)
        if i == 6:
            tile = jnp.concatenate([tile, third[:, 96:128]], axis=1)
        store_tile(i, tile)
    for d in FAR_W:
        to = lax.rem(aw + d, NX * NZ)
        remote(grads.at[to], part.at[aw], a_s, a_r, in_w(d)).start()

    squares = jnp.broadcast_to(jnp.sum(misfit * misfit, axis=0, keepdims=True), (8, 128))
    group = jnp.where(iota((128, 128), 0) // 16 == lanes128 % 8, 1.0, 0.0)
    l_send[...] = dot(squares, group, precision=HIGH)[0:1] / 384.0
    everyone(l_send, l_recv, l_s, l_r, ay, in_y, FAR_Y)
    l_recv[ay] = l_send[...]

    part[aw] = grads[aw]
    all_here(part, a_s, a_r)

    def added(buf):
        total = buf[0].astype(F32)
        for s in range(1, 16):
            total = total + buf[s].astype(F32)
        return total

    sum1[...] = added(part).astype(BF16)
    everyone(sum1, spread, b_s, b_r, ay, in_same, FAR_Y)
    spread[ay] = sum1[...]

    all_here(l_recv, l_s, l_r)
    lanes16 = iota((16, 128), 1)
    rank = jnp.zeros((16, 128), I32)
    for s in range(1, 8):
        earlier = (pltpu.roll(owned, s, 1) == owned) & (lanes16 % 8 >= s)
        rank = rank + jnp.where(earlier, 1, 0)
    losses = l_recv[:, 0, :]
    own = (owned == ay) & (lanes16 < 8)
    place = lanes16 - 2 * iota((16, 128), 0)
    slots = jnp.zeros((16, 128), F32)
    for r in range(2):
        value = jnp.sum(jnp.where(own & (rank == r), losses, 0.0), axis=1, keepdims=True)
        slots = slots + jnp.where(place == r, value, 0.0)
    loss_out[...] = jnp.sum(slots, axis=0, keepdims=True)[:, 0:32]
    write_loss = pltpu.make_async_copy(loss_out, loss_hbm, local_sem.at[8])
    write_loss.start()

    all_here(spread, b_s, b_r)
    sum2[...] = added(spread).astype(BF16)
    everyone(sum2, final, c_s, c_r, aw, in_w, FAR_W)
    own_part = pltpu.make_async_copy(sum2, final.at[aw], local_sem.at[9])
    own_part.start()
    write.wait()
    write_loss.wait()
    own_part.wait()
    for buf, s, r in (
        (t_recv, t_s, t_r), (l_recv, l_s, l_r), (part, a_s, a_r), (spread, b_s, b_r),
        (final, c_s, c_r),
    ):
        all_sent(buf, s, r)
    all_here(final, c_s, c_r)


def hand_over_kernel(
    adv_in, loss_in, final_in, adv_out, loss_out, first_out, second_out, third_out,
    adv, loss, final, first, second, third, sem,
):
    load_final = pltpu.make_async_copy(final_in, final, sem.at[5])
    load_final.start()
    pieces = [(c, slice(4 * h, 4 * h + 4)) for c in range(4) for h in range(2)]
    loads = [
        pltpu.make_async_copy(adv_in.at[piece], adv.at[piece], sem.at[6 + i])
        for i, piece in enumerate(pieces)
    ]
    loads.append(pltpu.make_async_copy(loss_in, loss, sem.at[4]))
    for load in loads:
        load.start()
    load_final.wait()
    for i in range(6):
        second[:, 128 * i : 128 * i + 128] = final[2 * i : 2 * i + 2].astype(F32).reshape(32, 128)
    last = final[12:14].astype(F32).reshape(32, 128)
    second[:, 768:864] = last[:, 0:96]
    third[...] = last[0:6, 96:128]
    first[...] = final[14:16].astype(F32).reshape(32, 128)[:, 0:108]
    stores = [
        pltpu.make_async_copy(second, second_out, sem.at[0]),
        pltpu.make_async_copy(first, first_out, sem.at[1]),
        pltpu.make_async_copy(third, third_out, sem.at[2]),
    ]
    for store in stores:
        store.start()
    for i, piece in enumerate(pieces):
        loads[i].wait()
        stores.append(pltpu.make_async_copy(adv.at[piece], adv_out.at[piece], sem.at[14 + i]))
        stores[-1].start()
    loads[8].wait()
    stores.append(pltpu.make_async_copy(loss, loss_out, sem.at[3]))
    stores[-1].start()
    for store in stores:
        store.wait()


def on_device(fields, viscosity, samples, trainers, conv_first, conv_second, conv_third):
    hbm = pl.BlockSpec(memory_space=pl.ANY)
    dma = pltpu.SemaphoreType.DMA
    v = pltpu.VMEM
    shapes = (
        jax.ShapeDtypeStruct((4, 8, 32, 128), F32),
        jax.ShapeDtypeStruct((1, 32), F32),
        jax.ShapeDtypeStruct((32, 108), F32),
        jax.ShapeDtypeStruct((32, 864), F32),
        jax.ShapeDtypeStruct((6, 32), F32),
    )
    results = pl.pallas_call(
        whole_kernel,
        out_shape=(shapes[0], shapes[1], jax.ShapeDtypeStruct((16, 16, 128), BF16)),
        in_specs=[hbm] * 7,
        out_specs=(hbm,) * 3,
        scratch_shapes=[
            pltpu.SMEM((8,), I32), pltpu.SMEM((8,), I32),
            v((5, 10, 32, 128), F32), v((4, 10, 32, 128), F32), v((4, 8, 32, 128), F32),
            v((2, 5, 8, 128), F32), v((2, 5, 8, 128), F32),
            v((2, 16, 128), F32), v((2, 16, 128), F32),
            v((2, 4, 8, 128), F32), v((2, 4, 8, 128), F32),
            v((2, 8, 128), F32), v((2, 8, 128), F32),
            v((1, 128), I32), v((16, 1, 128), I32), v((1, 128), F32), v((16, 1, 128), F32),
            v((32, 108), BF16), v((32, 864), BF16), v((6, 32), BF16),
            v((864, 32), BF16), v((128, 256), BF16), v((128, 128), F32), v((4, 64, 128), BF16),
            v((128, 512), F32), v((864, 512), BF16),
            v((16, 16, 128), BF16), v((16, 16, 128), BF16), v((16, 128), BF16),
            v((16, 16, 128), BF16), v((16, 128), BF16), v((1, 32), F32),
            dma((10,)),
            dma((2,)), dma((2,)), dma((2,)), dma((2,)), dma, dma,
            dma((2,)), dma((2,)), dma((2,)), dma((2,)), dma, dma,
            dma, dma, dma, dma, dma, dma, dma, dma, dma, dma,
        ],
        compiler_params=pltpu.CompilerParams(
            collective_id=0, has_side_effects=True, vmem_limit_bytes=60 * 1024 * 1024
        ),
        name="step",
    )(
        fields, viscosity, samples.reshape(8), trainers.reshape(8),
        conv_first, conv_second, conv_third,
    )
    advanced, losses, first, second, third = pl.pallas_call(
        hand_over_kernel,
        out_shape=shapes,
        in_specs=[hbm] * 3,
        out_specs=(hbm,) * 5,
        scratch_shapes=[
            v((4, 8, 32, 128), F32), v((1, 32), F32), v((16, 16, 128), BF16),
            v((32, 108), F32), v((32, 864), F32), v((6, 32), F32), dma((22,)),
        ],
        compiler_params=pltpu.CompilerParams(vmem_limit_bytes=60 * 1024 * 1024),
        name="hand_over",
    )(*results)
    return advanced, losses.reshape(1, 1, 1, 32), first, second, third


def solution(mesh):
    in_specs = (
        P(None, "gx", "gy", "gz"),
        P("gx", "gy", "gz"),
        P("gx", "gy", "gz", None),
        P("gx", "gy", "gz", None, None),
        P(),
        P(),
        P(),
    )
    out_specs = (P(None, "gx", "gy", "gz"), P("gx", "gy", "gz", None), P(), P(), P())
    return jax.shard_map(
        on_device, mesh=mesh, in_specs=in_specs, out_specs=out_specs, check_vma=False
    )
```

```python
import jax
import jax.numpy as jnp
from jax import lax
from jax.experimental import pallas as pl
from jax.experimental.pallas import tpu as pltpu
from jax.sharding import PartitionSpec as P

MESH = pl.DeviceIdType.MESH
F32 = jnp.float32
BF16 = jnp.bfloat16
I32 = jnp.int32
HIGH = lax.Precision.HIGHEST

NX, NY, NZ = 8, 16, 2
WORKERS = NX * NY * NZ
NT = (((1,), (1,)), ((), ()))
TN = (((0,), (0,)), ((), ()))
TIME_STEP = 0.25
BUOYANCY = 0.5
FAR_Y = (4, 12, 3, 5, 11, 13, 2, 6, 10, 14, 1, 7, 9, 15, 8)
FAR_W = (8, 9, 10, 7, 11, 6, 5, 4, 12, 13, 14, 3, 2, 15, 1)
PAIR_P = (0, 1, 2, 0, 0, 1)
PAIR_Q = (0, 1, 2, 1, 2, 2)


def iota(shape, dim):
    return lax.broadcasted_iota(I32, shape, dim)


def flux(low, high, visc_low, visc_high, d):
    speed = 0.25 * (low[d] + high[d])
    visc = 0.5 * (visc_low + visc_high)
    return [speed * (a + b) - visc * (b - a) for a, b in zip(low, high)]


def inner_part(src, visc, store):
    rows = iota((32, 128), 0)
    lanes = iota((32, 128), 1)

    def plane(p, before, is_last):
        q = [src[c, p] for c in range(4)]
        v = visc(p)
        if is_last:
            after = None
            total = [-b for b in before]
        else:
            after = flux(q, [src[c, p + 1] for c in range(4)], v, visc(p + 1), 0)
            total = after if before is None else [a - b for a, b in zip(after, before)]
        for axis, size, edge, d in ((0, 32, rows == 31, 1), (1, 128, lanes == 127, 2)):
            q_next = [pltpu.roll(x, size - 1, axis) for x in q]
            faces = flux(q, q_next, v, pltpu.roll(v, size - 1, axis), d)
            faces = [jnp.where(edge, 0.0, f) for f in faces]
            total = [t + (f - pltpu.roll(f, 1, axis)) for t, f in zip(total, faces)]
        out = [x - TIME_STEP * t for x, t in zip(q, total)]
        out[2] = out[2] + (TIME_STEP * BUOYANCY) * q[3]
        store(p, out)
        return after

    def body(p, before):
        return tuple(plane(p, before, False))

    before = lax.fori_loop(2, 8, body, tuple(plane(1, None, False)))
    plane(8, before, True)


def edge_z(dst, first, z_own, z_far, v_own, v_far):
    rows = iota((128, 128), 0)

    def face(ref, side):
        return [ref[side, 2 * c : 2 * c + 2] for c in range(4)]

    low = flux(face(z_far, 1), face(z_own, 0), v_far[1, 8:10], v_own[0, 8:10], 2)
    high = flux(face(z_own, 1), face(z_far, 0), v_own[1, 8:10], v_far[0, 8:10], 2)
    for c in range(4):
        for h in range(2):
            placed = jnp.where(
                rows == 0,
                TIME_STEP * low[c][h : h + 1],
                jnp.where(rows == 127, -TIME_STEP * high[c][h : h + 1], 0.0),
            )
            planes = slice(first + 4 * h, first + 4 * h + 4)
            dst[c, planes] = dst[c, planes] + placed.T.reshape(4, 32, 128)


def edge_x(src, visc, dst, first):
    def of(p):
        return [src[c, p] for c in range(4)]

    low = flux(of(0), of(1), visc(0), visc(1), 0)
    high = flux(of(8), of(9), visc(8), visc(9), 0)
    for c in range(4):
        dst[c, first] = dst[c, first] + TIME_STEP * low[c]
        dst[c, first + 7] = dst[c, first + 7] - TIME_STEP * high[c]


def edge_y(dst, first, y_own, y_far, v_own, v_far):
    def face(ref, side):
        return [ref[side, c] for c in range(4)]

    low = flux(face(y_far, 0), face(y_own, 0), v_far[0, 4], v_own[0, 4], 1)
    high = flux(face(y_own, 1), face(y_far, 1), v_own[1, 4], v_far[1, 4], 1)
    planes = slice(first, first + 8)
    for c in range(4):
        dst[c, planes, 0, :] = dst[c, planes, 0, :] + TIME_STEP * low[c]
        dst[c, planes, 31, :] = dst[c, planes, 31, :] - TIME_STEP * high[c]


def pack_y(src, count, y_send):
    for c in range(count):
        y_send[0, c] = src[c, 1:9, 0, :]
        y_send[1, c] = src[c, 1:9, 31, :]


def pack_z(src, count, z_send):
    for c in range(count):
        for h in range(2):
            turned = src[c, 1 + 4 * h : 5 + 4 * h].reshape(128, 128).T
            g = 2 * c + h
            z_send[0, g : g + 1, :] = turned[0:1]
            z_send[1, g : g + 1, :] = turned[127:128]


def by_lane(values, lanes_of):
    out = jnp.zeros(lanes_of.shape, I32)
    for j in range(8):
        out = jnp.where(lanes_of == j, values[j], out)
    return out


def shifts():
    return [(ox, oy) for ox in (-1, 0, 1) for oy in (-1, 0, 1)]


def inside(ox, oy):
    lanes = iota((1, 128), 1)
    x = lanes // 4 % 4 + ox
    y = lanes % 4 + oy
    return jnp.where((x >= 0) & (x < 4) & (y >= 0) & (y < 4), 1.0, 0.0)


def rolled(x, ox, oy):
    if ox == 0 and oy == 0:
        return x
    return pltpu.roll(x, (-(4 * ox + oy)) % 128, 1) * inside(ox, oy)


def box(x):
    rows = iota(x.shape, 0) % 4
    lanes = iota(x.shape, 1)
    count = x.shape[0]
    x = (
        x
        + jnp.where(rows > 0, pltpu.roll(x, 1, 0), 0.0)
        + jnp.where(rows < 3, pltpu.roll(x, count - 1, 0), 0.0)
    )
    for step, place in ((1, lanes % 4), (4, lanes // 4 % 4)):
        x = (
            x
            + jnp.where(place > 0, pltpu.roll(x, step, 1), 0.0)
            + jnp.where(place < 3, pltpu.roll(x, 128 - step, 1), 0.0)
        )
    return x / 27.0


def cat_rows(x):
    return jnp.concatenate([x[:, 128 * z : 128 * z + 128] for z in range(4)], axis=0)


def dot(a, b, dims=None, precision=None):
    if dims is None:
        dims = (((1,), (0,)), ((), ()))
    return lax.dot_general(a, b, dims, precision=precision, preferred_element_type=F32)


def whole_kernel(
    fields_hbm, visc_hbm, samples_hbm, trainers_hbm, w1_hbm, w2_hbm, w3_hbm,
    adv_hbm, loss_hbm, final,
    samples, trainers,
    start, mid, adv, y_send, y_recv, z_send, z_recv, y_send2, y_recv2, z_send2, z_recv2,
    t_send, t_recv, l_send, l_recv, w1, w2, w3, w2_turned, hot, keep, folds, st1, st2,
    grads, part, sum1, spread, sum2, loss_out,
    local_sem, x_s, x_r, y_s, y_r, z_s, z_r, x2_s, x2_r, y2_s, y2_r, z2_s, z2_r,
    t_s, t_r, l_s, l_r, a_s, a_r, b_s, b_r, c_s, c_r,
):
    ax = lax.axis_index("gx")
    ay = lax.axis_index("gy")
    az = lax.axis_index("gz")
    half = ay // 8
    az_seen = lax.rem(az + half, 2)
    aw = ax * NZ + az_seen

    def in_same(d):
        to = lax.rem(ay + d, NY)
        return (ax, to, lax.rem(az_seen + to // 8, 2))

    def in_y(d):
        return (ax, lax.rem(ay + d, NY), az)

    def in_w(d):
        w = lax.rem(aw + d, NX * NZ)
        return (w // NZ, ay, lax.rem(w + half, NZ))

    loads = [
        pltpu.make_async_copy(src, dst, local_sem.at[i])
        for i, (src, dst) in enumerate(
            (
                (fields_hbm, start.at[0:4, 1:9]),
                (visc_hbm, start.at[4, 1:9]),
                (trainers_hbm, trainers),
                (samples_hbm, samples),
                (w1_hbm, w1),
                (w2_hbm, w2),
                (w3_hbm, w3),
            )
        )
    ]
    loads[0].start()
    loads[1].start()
    barrier = pltpu.get_barrier_semaphore()

    def greet(d, carry):
        pl.semaphore_signal(barrier, inc=1, device_id=in_y(d), device_id_type=MESH)
        pl.semaphore_signal(barrier, inc=1, device_id=in_w(d), device_id_type=MESH)
        return carry

    lax.fori_loop(1, 16, greet, 0)

    def greet_mirrored(d, carry):
        to = lax.rem((1 - half) * 8 + d, NY)
        pl.semaphore_signal(barrier, inc=1, device_id=(ax, to, 1 - az), device_id_type=MESH)
        return carry

    lax.fori_loop(0, 8, greet_mirrored, 0)
    for load in loads[2:]:
        load.start()
    loads[0].wait()
    loads[1].wait()
    pack_y(start, 5, y_send)
    pack_z(start, 5, z_send)
    loads[2].wait()
    owners = [trainers[j] for j in range(8)]
    t_send[...] = by_lane(owners, iota((1, 128), 1) % 8)
    pl.semaphore_wait(barrier, 38)

    def remote(src, dst, s, r, to):
        return pltpu.make_async_remote_copy(
            src_ref=src, dst_ref=dst, send_sem=s, recv_sem=r, device_id=to, device_id_type=MESH
        )

    x_up = (lax.rem(ax + 1, NX), ay, az)
    x_down = (lax.rem(ax + NX - 1, NX), ay, az)
    other = (ax, ay, 1 - az)

    def exchange_x(ref, s, r):
        return [
            remote(ref.at[:, 8], ref.at[:, 0], s.at[0], r.at[0], x_up),
            remote(ref.at[:, 1], ref.at[:, 9], s.at[1], r.at[1], x_down),
        ]

    def exchange_y(ys, yr, s, r):
        return [
            remote(ys.at[1], yr.at[0], s.at[0], r.at[0], in_y(1)),
            remote(ys.at[0], yr.at[1], s.at[1], r.at[1], in_y(NY - 1)),
        ]

    def begin(moves):
        for move in moves:
            move.start()

    leaving = []

    def finish(moves):
        for move in moves:
            move.wait_recv()
        leaving.extend(moves)

    def everyone(src, buf, s, r, slot, to, order):
        for d in order:
            remote(src, buf.at[slot], s, r, to(d)).start()

    def all_here(buf, s, r):
        others = buf.at[pl.ds(0, 15)]
        remote(others, others, s, r, other).wait_recv()

    def all_sent(buf, s, r):
        others = buf.at[pl.ds(0, 15)]
        remote(others, others, s, r, other).wait_send()

    moves_y = exchange_y(y_send, y_recv, y_s, y_r)
    moves_x = exchange_x(start, x_s, x_r)
    moves_z = [remote(z_send, z_recv, z_s, z_r, other)]
    begin(moves_y)
    begin(moves_x)
    begin(moves_z)
    everyone(t_send, t_recv, t_s, t_r, ay, in_y, FAR_Y)
    t_recv[ay] = t_send[...]

    def visc(p):
        return start[4, p]

    def store_mid(p, out):
        for c in range(4):
            mid[c, p] = out[c]

    inner_part(start, visc, store_mid)
    loads[3].wait()
    picked = [samples[j] for j in range(8)]
    row = iota((128, 256), 0)
    base = by_lane([(s // 256) * 128 + (s // 32 % 8) * 4 for s in picked], row // 16)
    want = base + row // 4 % 4 * 32 + row % 4
    hot[...] = jnp.where(want == iota((128, 256), 1), 1.0, 0.0).astype(BF16)
    lanes128 = iota((128, 128), 1)
    lz = by_lane([s % 32 for s in picked], iota((128, 128), 0) // 16)
    keep[...] = jnp.where(lz == lanes128 // 4, 1.0, 0.0)
    finish(moves_z)
    edge_z(mid, 1, z_send, z_recv, z_send, z_recv)
    finish(moves_x)
    edge_x(start, visc, mid, 1)
    finish(moves_y)
    edge_y(mid, 1, y_send, y_recv, y_send, y_recv)

    pack_y(mid, 4, y_send2)
    moves_y = exchange_y(y_send2, y_recv2, y2_s, y2_r)
    begin(moves_y)
    moves_x = exchange_x(mid, x2_s, x2_r)
    begin(moves_x)
    pack_z(mid, 4, z_send2)
    moves_z = [remote(z_send2, z_recv2, z2_s, z2_r, other)]
    begin(moves_z)

    def store_adv(p, out):
        for c in range(4):
            adv[c, p - 1] = out[c]

    inner_part(mid, visc, store_adv)
    frow = iota((64, 128), 0)
    flane = iota((64, 128), 1)
    comp = frow % 4
    for i, c in enumerate(PAIR_P + PAIR_Q):
        here = (frow >= 16 + 4 * i) & (frow < 20 + 4 * i)
        comp = jnp.where(here, c, comp)
    zrow = jnp.where(frow < 16, frow // 4, frow % 4)
    for c in range(4):
        folds[c] = jnp.where((comp == c) & (flane % 4 == zrow), 1.0, 0.0).astype(BF16)
    for load in loads[4:]:
        load.wait()
    st1[...] = jnp.zeros_like(st1)
    st2[...] = jnp.zeros_like(st2)
    for t in range(7):
        width = 128 if t < 6 else 96
        turned = w2[:, 128 * t : 128 * t + width].astype(F32).T
        w2_turned[128 * t : 128 * t + width, :] = turned.astype(BF16)
    pick_row = jnp.where(iota((24, 6), 0) // 4 == iota((24, 6), 1), 1.0, 0.0).astype(BF16)
    pick_col = jnp.where(iota((32, 128), 1) % 32 == iota((32, 128), 0), 1.0, 0.0).astype(BF16)
    spread3 = dot(dot(pick_row, w3[...]).astype(BF16), pick_col)
    same_z = iota((24, 128), 0) % 4 == iota((24, 128), 1) // 32
    wide3 = jnp.where(same_z, spread3, 0.0).astype(BF16)
    all_here(t_recv, t_s, t_r)
    owned = t_recv[:, 0, :]
    mine = by_lane(owners, iota((16, 128), 1) // 16)
    load = jnp.zeros((16, 128), F32)
    for s in range(8):
        other_owner = owned if s == 0 else pltpu.roll(owned, s, 1)
        load = load + jnp.where(other_owner == mine, 1.0, 0.0)
    load = jnp.sum(load, axis=0, keepdims=True)
    share = 1.0 / (WORKERS * jnp.maximum(load, 1.0))
    scale = share * (2.0 / 384.0)
    finish(moves_z)
    edge_z(adv, 0, z_send2, z_recv2, z_send, z_recv)
    finish(moves_x)
    edge_x(mid, visc, adv, 0)
    finish(moves_y)
    edge_y(adv, 0, y_send2, y_recv2, y_send, y_recv)
    write = pltpu.make_async_copy(adv, adv_hbm, local_sem.at[7])
    write.start()

    cells = jnp.zeros((64, 128), F32)
    for c in range(4):
        plane = adv[c].reshape(256, 128).astype(BF16)
        found = (dot(hot[...], plane) * keep[...]).astype(BF16)
        cells = cells + dot(folds[c], found, NT)

    chosen = cells[0:16]
    for i, (ox, oy) in enumerate(shifts()):
        moved = rolled(chosen, ox, oy)
        for o in range(3):
            k = 3 * i + o
            for z in range(4):
                if 0 <= z + o - 1 < 4:
                    st1[4 * k : 4 * k + 4, 128 * z : 128 * z + 128] = moved[
                        4 * (z + o - 1) : 4 * (z + o - 1) + 4
                    ]
    pre1 = cat_rows(dot(w1[...], st1[0:108, :].astype(BF16)))
    sig1 = jax.nn.sigmoid(pre1)
    slope1 = sig1 * (1.0 + pre1 * (1.0 - sig1))
    hid1 = (pre1 * sig1).astype(BF16).astype(F32)
    for i, (ox, oy) in enumerate(shifts()):
        moved = rolled(hid1, ox, oy).astype(BF16)
        for o in range(3):
            k = 3 * i + o
            for z in range(4):
                if 0 <= z + o - 1 < 4:
                    st2[32 * k : 32 * k + 32, 128 * z : 128 * z + 128] = moved[
                        32 * (z + o - 1) : 32 * (z + o)
                    ]
    pre2 = cat_rows(dot(w2[...], st2[0:864, :]))
    sig2 = jax.nn.sigmoid(pre2)
    slope2 = sig2 * (1.0 + pre2 * (1.0 - sig2))
    hid2 = (pre2 * sig2).astype(BF16)
    predicted = dot(wide3, hid2)
    up_p, up_q = cells[16:40], cells[40:64]
    smooth = box(jnp.concatenate([up_p * up_q, up_p, up_q], axis=0))
    misfit = predicted - (smooth[0:24] - smooth[24:48] * smooth[48:72])
    grad_pred = (misfit * scale).astype(BF16)

    third = jnp.where(same_z, dot(grad_pred, hid2, NT), 0.0)
    third = jnp.concatenate(
        [jnp.sum(third[4 * i : 4 * i + 4], axis=0, keepdims=True) for i in range(6)]
        + [jnp.zeros((26, 128), F32)],
        axis=0,
    )
    third = third + pltpu.roll(third, 32, 1)
    third = third + pltpu.roll(third, 64, 1)
    grad_mid = (dot(wide3, grad_pred, TN) * slope2).astype(BF16)
    mid_cols = jnp.concatenate([grad_mid[32 * z : 32 * z + 32] for z in range(4)], axis=1)

    def store_tile(i, x):
        grads[2 * i] = x[0:16].astype(BF16)
        grads[2 * i + 1] = x[16:32].astype(BF16)

    lower = jnp.zeros((128, 128), F32)
    for i, (ox, oy) in enumerate(shifts()):
        y = dot(w2_turned[96 * i : 96 * i + 96, :], mid_cols)
        parts = []
        for z in range(4):
            total = y[32:64, 128 * z : 128 * z + 128]
            if z + 1 < 4:
                total = total + y[0:32, 128 * z + 128 : 128 * z + 256]
            if z - 1 >= 0:
                total = total + y[64:96, 128 * z - 128 : 128 * z]
            parts.append(total)
        lower = lower + rolled(jnp.concatenate(parts, axis=0), -ox, -oy)
    entry = (lower * slope1).astype(BF16)
    entry_cols = jnp.concatenate([entry[32 * z : 32 * z + 32] for z in range(4)], axis=1)
    store_tile(7, dot(entry_cols, st1[...].astype(BF16), NT))
    for i in range(7):
        rows_here = 128 if i < 6 else 96
        tile = dot(mid_cols, st2[128 * i : 128 * i + rows_here, :], NT)
        if i == 6:
            tile = jnp.concatenate([tile, third[:, 96:128]], axis=1)
        store_tile(i, tile)
    for d in FAR_W:
        to = lax.rem(aw + d, NX * NZ)
        remote(grads.at[to], part.at[aw], a_s, a_r, in_w(d)).start()

    squares = jnp.broadcast_to(jnp.sum(misfit * misfit, axis=0, keepdims=True), (8, 128))
    group = jnp.where(iota((128, 128), 0) // 16 == lanes128 % 8, 1.0, 0.0)
    l_send[...] = dot(squares, group, precision=HIGH)[0:1] / 384.0
    everyone(l_send, l_recv, l_s, l_r, ay, in_y, FAR_Y)
    l_recv[ay] = l_send[...]

    part[aw] = grads[aw]
    all_here(part, a_s, a_r)

    def added(buf):
        total = buf[0].astype(F32)
        for s in range(1, 16):
            total = total + buf[s].astype(F32)
        return total

    sum1[...] = added(part).astype(BF16)
    everyone(sum1, spread, b_s, b_r, ay, in_same, FAR_Y)
    spread[ay] = sum1[...]

    all_here(l_recv, l_s, l_r)
    lanes16 = iota((16, 128), 1)
    rank = jnp.zeros((16, 128), I32)
    for s in range(1, 8):
        earlier = (pltpu.roll(owned, s, 1) == owned) & (lanes16 % 8 >= s)
        rank = rank + jnp.where(earlier, 1, 0)
    losses = l_recv[:, 0, :]
    own = (owned == ay) & (lanes16 < 8)
    place = lanes16 - 2 * iota((16, 128), 0)
    slots = jnp.zeros((16, 128), F32)
    for r in range(2):
        value = jnp.sum(jnp.where(own & (rank == r), losses, 0.0), axis=1, keepdims=True)
        slots = slots + jnp.where(place == r, value, 0.0)
    loss_out[...] = jnp.sum(slots, axis=0, keepdims=True)[:, 0:32]
    write_loss = pltpu.make_async_copy(loss_out, loss_hbm, local_sem.at[8])
    write_loss.start()

    all_here(spread, b_s, b_r)
    sum2[...] = added(spread).astype(BF16)
    everyone(sum2, final, c_s, c_r, aw, in_w, FAR_W)
    own_part = pltpu.make_async_copy(sum2, final.at[aw], local_sem.at[9])
    own_part.start()
    write.wait()
    write_loss.wait()
    own_part.wait()
    for buf, s, r in (
        (t_recv, t_s, t_r), (l_recv, l_s, l_r), (part, a_s, a_r), (spread, b_s, b_r),
        (final, c_s, c_r),
    ):
        all_sent(buf, s, r)
    for move in leaving:
        move.wait_send()
    all_here(final, c_s, c_r)


def hand_over_kernel(
    adv_in, loss_in, final_in, adv_out, loss_out, first_out, second_out, third_out,
    adv, loss, final, first, second, third, sem,
):
    load_final = pltpu.make_async_copy(final_in, final, sem.at[5])
    load_final.start()
    pieces = [(c, slice(4 * h, 4 * h + 4)) for c in range(4) for h in range(2)]
    loads = [
        pltpu.make_async_copy(adv_in.at[piece], adv.at[piece], sem.at[6 + i])
        for i, piece in enumerate(pieces)
    ]
    loads.append(pltpu.make_async_copy(loss_in, loss, sem.at[4]))
    for load in loads:
        load.start()
    load_final.wait()
    for i in range(6):
        second[:, 128 * i : 128 * i + 128] = final[2 * i : 2 * i + 2].astype(F32).reshape(32, 128)
    last = final[12:14].astype(F32).reshape(32, 128)
    second[:, 768:864] = last[:, 0:96]
    third[...] = last[0:6, 96:128]
    first[...] = final[14:16].astype(F32).reshape(32, 128)[:, 0:108]
    stores = [
        pltpu.make_async_copy(second, second_out, sem.at[0]),
        pltpu.make_async_copy(first, first_out, sem.at[1]),
        pltpu.make_async_copy(third, third_out, sem.at[2]),
    ]
    for store in stores:
        store.start()
    for i, piece in enumerate(pieces):
        loads[i].wait()
        stores.append(pltpu.make_async_copy(adv.at[piece], adv_out.at[piece], sem.at[14 + i]))
        stores[-1].start()
    loads[8].wait()
    stores.append(pltpu.make_async_copy(loss, loss_out, sem.at[3]))
    stores[-1].start()
    for store in stores:
        store.wait()


def on_device(fields, viscosity, samples, trainers, conv_first, conv_second, conv_third):
    hbm = pl.BlockSpec(memory_space=pl.ANY)
    dma = pltpu.SemaphoreType.DMA
    v = pltpu.VMEM
    shapes = (
        jax.ShapeDtypeStruct((4, 8, 32, 128), F32),
        jax.ShapeDtypeStruct((1, 32), F32),
        jax.ShapeDtypeStruct((32, 108), F32),
        jax.ShapeDtypeStruct((32, 864), F32),
        jax.ShapeDtypeStruct((6, 32), F32),
    )
    results = pl.pallas_call(
        whole_kernel,
        out_shape=(shapes[0], shapes[1], jax.ShapeDtypeStruct((16, 16, 128), BF16)),
        in_specs=[hbm] * 7,
        out_specs=(hbm,) * 3,
        scratch_shapes=[
            pltpu.SMEM((8,), I32), pltpu.SMEM((8,), I32),
            v((5, 10, 32, 128), F32), v((4, 10, 32, 128), F32), v((4, 8, 32, 128), F32),
            v((2, 5, 8, 128), F32), v((2, 5, 8, 128), F32),
            v((2, 16, 128), F32), v((2, 16, 128), F32),
            v((2, 4, 8, 128), F32), v((2, 4, 8, 128), F32),
            v((2, 8, 128), F32), v((2, 8, 128), F32),
            v((1, 128), I32), v((16, 1, 128), I32), v((1, 128), F32), v((16, 1, 128), F32),
            v((32, 108), BF16), v((32, 864), BF16), v((6, 32), BF16),
            v((864, 32), BF16), v((128, 256), BF16), v((128, 128), F32), v((4, 64, 128), BF16),
            v((128, 512), F32), v((864, 512), BF16),
            v((16, 16, 128), BF16), v((16, 16, 128), BF16), v((16, 128), BF16),
            v((16, 16, 128), BF16), v((16, 128), BF16), v((1, 32), F32),
            dma((10,)),
            dma((2,)), dma((2,)), dma((2,)), dma((2,)), dma, dma,
            dma((2,)), dma((2,)), dma((2,)), dma((2,)), dma, dma,
            dma, dma, dma, dma, dma, dma, dma, dma, dma, dma,
        ],
        compiler_params=pltpu.CompilerParams(
            collective_id=0, has_side_effects=True, vmem_limit_bytes=60 * 1024 * 1024
        ),
        name="step",
    )(
        fields, viscosity, samples.reshape(8), trainers.reshape(8),
        conv_first, conv_second, conv_third,
    )
    advanced, losses, first, second, third = pl.pallas_call(
        hand_over_kernel,
        out_shape=shapes,
        in_specs=[hbm] * 3,
        out_specs=(hbm,) * 5,
        scratch_shapes=[
            v((4, 8, 32, 128), F32), v((1, 32), F32), v((16, 16, 128), BF16),
            v((32, 108), F32), v((32, 864), F32), v((6, 32), F32), dma((22,)),
        ],
        compiler_params=pltpu.CompilerParams(vmem_limit_bytes=60 * 1024 * 1024),
        name="hand_over",
    )(*results)
    return advanced, losses.reshape(1, 1, 1, 32), first, second, third


def solution(mesh):
    in_specs = (
        P(None, "gx", "gy", "gz"),
        P("gx", "gy", "gz"),
        P("gx", "gy", "gz", None),
        P("gx", "gy", "gz", None, None),
        P(),
        P(),
        P(),
    )
    out_specs = (P(None, "gx", "gy", "gz"), P("gx", "gy", "gz", None), P(), P(), P())
    return jax.shard_map(
        on_device, mesh=mesh, in_specs=in_specs, out_specs=out_specs, check_vma=False
    )
```
